32 devices in a mesh: rows: 8 (over z, x), rep: 4 (over y, core).
Axes of the slice: x: 2, y: 2, z: 4, core: 2. Of those that a mesh axis runs over, the one named last changes fastest.
Arguments:
- right_side: float32 [32768, 1024], P(('rep', 'rows')), parts along dimension 0, may hold values from -6 to 6
- leaf_inverse: float32 [32768, 256], P(('rep', 'rows')), parts along dimension 0, may hold values from -0.375 to 0.375
- left_factors: float32 [5, 32768, 64], P(None, ('rep', 'rows')), parts along dimension 1, may hold values from -0.75 to 0.75
- right_factors: float32 [5, 32768, 64], P(None, ('rep', 'rows')), parts along dimension 1, may hold values from -0.4375 to 0.4375, as said below
- cores: float32 [124, 128, 128], P('rep'), parts along dimension 0, may hold values from -0.5 to 0.5
Outputs:
- solution: float32 [32768, 1024], P(('rep', 'rows')), parts along dimension 0
The draws below stay inside these ranges and needn't reach their ends.
There are 4 independent parts, one for each index of `rep`. The reference program is written for one: setup_inputs(seed, part) draws one part's arguments, and reference() takes and returns one part's arrays. A program takes and returns all parts, laid end to end along the dimension named above; each array names one. Nothing has to cross between parts.
Inputs may be any that keep to these rules, and one draw needn't show every extreme that they name: `right_factors`: level j's entries are of order (8192 / 2^(j+1))^(-1/2).
All inputs are finite; a program needn't handle non-finite values.
Results may differ from the reference program's by a relative error of at most 0.00016.
Values sent between devices are 32-bit elements; how exact they have to be, the bound alone decides.
A program may use at most 128 MiB of HBM per device.

```python
import jax
import jax.numpy as jnp
from jax import lax

COLS = 1024
RANK = 64
LEVELS = 5
NTOT = 8192
LEAF = 256
NODES = 31


def draw_right_factors(key, part):
    depth = jnp.arange(LEVELS).astype(jnp.float32)
    scale = (NTOT / 2.0 ** (depth + 1.0)) ** (-0.5)
    normal = jax.random.truncated_normal(key, -6.0, 6.0, (LEVELS, NTOT, RANK), jnp.float32)
    return normal * scale[:, None, None]


def steps_of(key, extent, cuts, smallest, largest):
    def one(dim, blocks):
        heights = jax.random.uniform(jax.random.fold_in(jax.random.fold_in(key, 6), dim), (blocks,), jnp.float32, smallest / len(cuts), largest / len(cuts))
        return jnp.repeat(jnp.exp(heights), extent[dim] // blocks).reshape((-1,) + (1,) * (len(extent) - dim - 1))

    level = one(*cuts[0])
    for cut in cuts[1:]:
        level = level * one(*cut)
    return level


def normal_values(stream_key, dims, deviation, limit, cuts=(), kind=jnp.bfloat16):
    drawn = jax.random.normal(stream_key, dims, jnp.float32) * deviation
    if len(cuts) > 0:
        drawn = steps_of(stream_key, dims, cuts, -0.22, 0.18) * drawn
    return jnp.clip(drawn, min=-limit, max=limit).astype(kind)


def setup_inputs(seed: int = 0, part: int = 0) -> dict:
    key_list = jax.random.split(jax.random.key(seed), 6)
    own_keys = jax.random.split(jax.random.fold_in(key_list[5], part), 6)
    right_side = normal_values(own_keys[0], (NTOT, COLS), 1.0, 6.0, ((0, 8),), jnp.float32)
    leaf_inverse = normal_values(own_keys[1], (NTOT, LEAF), LEAF ** -0.5, 0.375, ((0, 8),), jnp.float32)
    left_factors = normal_values(own_keys[2], (LEVELS, NTOT, RANK), RANK ** -0.5, 0.75, ((1, 8),), jnp.float32)
    right_factors = draw_right_factors(jax.random.fold_in(jax.random.fold_in(key_list[5], part), 71), part)
    cores = normal_values(own_keys[4], (NODES, 2 * RANK, 2 * RANK), (2 * RANK) ** -0.5, 0.5, (), jnp.float32)
    return dict(right_side=right_side, leaf_inverse=leaf_inverse, left_factors=left_factors, right_factors=right_factors, cores=cores)


HIGH = lax.Precision.HIGHEST


def reference(right_side, leaf_inverse, left_factors, right_factors, cores):
    blocks = NTOT // LEAF
    solved = jnp.einsum("bij,bjk->bik", leaf_inverse.reshape(blocks, LEAF, LEAF), right_side.reshape(blocks, LEAF, COLS), precision=HIGH).reshape(NTOT, COLS)
    for level in reversed(range(LEVELS)):
        nodes = 2 ** level
        half = NTOT // nodes // 2
        shaped = solved.reshape(nodes, 2, half, COLS)
        basis_v = right_factors[level].reshape(nodes, 2, half, RANK)
        basis_u = left_factors[level].reshape(nodes, 2, half, RANK)
        projected = jnp.einsum("nchr,nchk->ncrk", basis_v, shaped, precision=HIGH)
        stacked = jnp.concatenate([projected[:, 1], projected[:, 0]], axis=1)
        core_set = cores[nodes - 1: 2 * nodes - 1]
        image = jnp.einsum("nst,ntk->nsk", core_set, stacked, precision=HIGH).reshape(nodes, 2, RANK, COLS)
        update = jnp.einsum("nchr,ncrk->nchk", basis_u, image, precision=HIGH)
        solved = (shaped - update).reshape(NTOT, COLS)
    return solved
```

```python
import contextlib
import functools

import jax
import jax.numpy as jnp
from jax import lax
from jax.experimental import pallas as pl
from jax.experimental.pallas import tpu as pltpu
from jax.sharding import PartitionSpec as P

LANES = 128
CHUNK = 2 * LANES
F32 = jnp.float32
BF16 = jnp.bfloat16
TREE_VMEM = 24 << 20
FINISH_VMEM = 12 << 20
MESH = pl.DeviceIdType.MESH
TRACE = False


def region(name):
    return jax.named_scope(name) if TRACE else contextlib.nullcontext()


def split(x):
    high = x.astype(BF16)
    return high, (x - high.astype(F32)).astype(BF16)


def level_order(bits, levels):
    return [bits - 1 - s for s in range(bits)] + list(range(bits, levels))


def local_offset(level, bits, rank):
    return rank * (2 ** (level - bits + 1) - 2)


def one(x, y, nt=False):
    dims = (((1,), (1 if nt else 0,)), ((), ()))
    return lax.dot_general(x, y, dims, preferred_element_type=F32)


def dot3(a, b, nt=False):
    return one(a[0], b[0], nt) + one(a[0], b[1], nt) + one(a[1], b[0], nt)


def dotk(a, b):
    return one(
        jnp.concatenate([a[0], a[0], a[1]], 1), jnp.concatenate([b[0], b[1], b[0]], 0)
    )


def dot(a, b):
    return dotk(split(a), split(b))


def swap_lanes(x):
    half = x.shape[1] // 2
    return jnp.concatenate([x[:, half:], x[:, :half]], 1)


def schedule(bits, chunks):
    if bits == 3 and chunks == 4:
        return [
            ("step", 0, 0), ("leaves", 0), ("step", 0, 1), ("leaves", 1),
            ("step", 1, 0), ("step", 0, 2), ("leaves", 2), ("step", 1, 1),
            ("step", 0, 3), ("step", 2, 0), ("step", 1, 2), ("leaves", 3),
            ("step", 2, 1), ("step", 1, 3), ("apply", 0), ("step", 2, 2),
            ("apply", 1), ("step", 2, 3), ("apply", 2),
        ]
    order = []
    for t in range(chunks + bits - 1):
        for s in range(bits):
            if 0 <= t - s < chunks:
                order.append(("step", s, t - s))
        if t < chunks:
            order.append(("leaves", t))
    return order + [("apply", c) for c in range(chunks - 1)]


def tree_kernel(bits, levels, blocks, right_hbm, leaf_hbm, vt_hbm, ut_hbm, cores_hbm, *refs):
    x_ref, q_last, u_high, u_low = refs[:4]
    rbuf, leaf, vt_ref, ut_ref, core_g, sem_in = refs[4:10]
    r_high, r_low, a_high, a_low, m_high, m_low, ql_ref = refs[10:17]
    op_high, op_low, gram_out, gram_in, keep, first_out, first_in = refs[17:24]
    later_out, later_in, q_out, q_all = refs[24:28]
    gram_sem, first_sem, later_sem, q_sem = refs[28:32]
    local_levels = list(range(bits, levels))
    core_l = refs[32 : 32 + len(local_levels)]
    ch_refs = refs[32 + len(local_levels) :]
    ch_refs = list(zip(ch_refs[::2], ch_refs[1::2]))

    me = lax.axis_index("rows")
    rank, rows_dev = vt_ref.shape[1:]
    chunks = rbuf.shape[0]
    lf = rows_dev // blocks
    half_id = lax.rem(me, 2)
    upper = half_id == 1
    order = level_order(bits, levels)
    gram_cols = gram_out.shape[2]

    def child(s):
        return lax.rem(me // 2**s, 2)

    def partner(s):
        return me + (1 - 2 * child(s)) * 2**s

    barrier = pltpu.get_barrier_semaphore()
    for s in range(bits):
        pl.semaphore_signal(
            barrier, inc=1, device_id={"rows": partner(s)}, device_id_type=MESH
        )

    slots = [0]

    def load(src, dst):
        copy = pltpu.make_async_copy(src, dst, sem_in.at[slots[0]])
        slots[0] += 1
        copy.start()
        return copy

    v_load = load(vt_hbm, vt_ref)
    leaf_load = load(leaf_hbm, leaf)
    u_load = load(ut_hbm, ut_ref)
    core_loads = []
    for n, level in enumerate(local_levels):
        count = 2 ** (level - bits)
        src = cores_hbm.at[pl.ds(2**level - 1 + me * count, count)]
        core_loads.append(load(src, core_l[n]))
    right_loads = [
        load(right_hbm.at[:, pl.ds(c * CHUNK, CHUNK)], rbuf.at[c]) for c in range(chunks)
    ]
    core_g_loads = []
    for s in range(bits):
        src = cores_hbm.at[2 ** (bits - 1 - s) - 1 + me // 2 ** (s + 1)]
        core_g_loads.append(load(src, core_g.at[s]))

    sent = []

    def send(src, dst, sems, s):
        copy = pltpu.make_async_remote_copy(
            src_ref=src,
            dst_ref=dst,
            send_sem=sems.at[0],
            recv_sem=sems.at[1],
            device_id={"rows": partner(s)},
            device_id_type=MESH,
        )
        copy.start()
        sent.append(copy)
        return copy

    with region("wait_v"):
        v_load.wait()
    vt = split(jnp.concatenate([vt_ref[level] for level in order], 0))
    with region("wait_leaf"):
        leaf_load.wait()
    with region("m"):
        high, low = split(leaf[...])
        a_high[:, :lf] = high
        a_low[:, :lf] = low
        for i in range(blocks):
            rows = slice(i * lf, (i + 1) * lf)
            high, low = split(
                dot3([v[:, rows] for v in vt], (a_high[rows, :lf], a_low[rows, :lf]))
            )
            m_high[i] = high
            m_low[i] = low
    with region("wait_u"):
        u_load.wait()
        for copy in core_loads:
            copy.wait()

    def set_local(n, k, gram):
        core = core_l[n][k]
        for ref, top, rest in zip(ch_refs[n], split(core), split(dot(gram, core))):
            ref[k, : 2 * rank] = top
            ref[k, 2 * rank :] = rest

    with region("grams"):
        fast = len(local_levels) == 2 and bits == 3 and 2 * rank == LANES
        if fast:
            ut = {level: split(ut_ref[level]) for level in range(1, levels)}
            rows_v = rank * (levels - 1)
            lane = lax.broadcasted_iota(jnp.int32, (rows_v, LANES), 1) < rank
            tile_a, tile_b = [], []
            for i in range(blocks):
                cols = slice(i * lf, (i + 1) * lf)
                names = [4, 2] if i % 2 == 0 else [2, 4]
                names += [3, 1] if i < 2 else [1, 3]
                rhs = [
                    jnp.concatenate([ut[level][j][:, cols] for level in names], 0)
                    for j in range(2)
                ]
                g = dot3([v[:rows_v, cols] for v in vt], rhs, nt=True)
                tile_a.append(g[:, :LANES])
                tile_b.append(g[:, LANES:])
            s01, s23 = tile_b[0] + tile_b[1], tile_b[2] + tile_b[3]
            even, odd = tile_a[0] + tile_a[2], tile_a[1] + tile_a[3]
            cut = slice(rank, rank * bits)
            gram_out[0] = jnp.where(
                lane[cut], odd[cut] + swap_lanes(even[cut]), s01[cut] + swap_lanes(s23[cut])
            )
        else:
            vr = [v[rank : rank * bits] for v in vt]
            ur = split(jnp.concatenate([ut_ref[level] for level in order], 0))
            gram_out[0] = dot3(vr, [u[:gram_cols] for u in ur], nt=True)
    with region("barrier"):
        pl.semaphore_wait(barrier, bits)
    gram_copy = {0: send(gram_out.at[0], gram_in.at[0], gram_sem.at[0], 0)}
    with region("ch"):
        if fast:
            for k in range(2):
                set_local(1, k, jnp.where(lane, tile_a[2 * k], tile_a[2 * k + 1]))
            cut = slice(0, rank * bits)
            set_local(0, 0, jnp.where(lane[cut], s01[cut], s23[cut]))
        else:
            for n, level in enumerate(local_levels):
                count = 2 ** (level - bits)
                node = rows_dev // count
                half = node // 2
                zero = jnp.zeros((rank, half), BF16)
                own = slice(rank * level, rank * (level + 1))
                for k in range(count):
                    base = k * node
                    diag = [
                        jnp.concatenate(
                            [
                                jnp.concatenate([u[own, base : base + half], zero], 1),
                                jnp.concatenate([zero, u[own, base + half : base + node]], 1),
                            ],
                            0,
                        )
                        for u in ur
                    ]
                    above = [v[: rank * level, base : base + node] for v in vt]
                    set_local(n, k, dot3(above, diag, nt=True))

    first_copy, later_copy, q_copy = {}, {}, {}

    def forward(c):
        right_loads[c].wait()
        high, low = split(rbuf[c])
        r_high[c] = high
        r_low[c] = low
        parts, later = [], []
        for i in range(blocks):
            rows = slice(i * lf, (i + 1) * lf)
            parts.append(dot3((m_high[i], m_low[i]), (r_high[c, rows, :], r_low[c, rows, :])))
        for n in reversed(range(len(local_levels))):
            level = local_levels[n]
            top = rank * level
            merged = []
            for k in range(len(parts) // 2):
                a, b = parts[2 * k], parts[2 * k + 1]
                both = split(jnp.concatenate([b[top:], a[top:]], 0))
                change = dotk([ref[k, 2 * rank :] for ref in ch_refs[n]], both)
                start = local_offset(level, bits, rank) + 2 * rank * k
                later.append((start, n, k, both))
                merged.append(a[:top] + b[:top] - change)
            parts = merged
        p = parts[0]
        low, high = p[:, :LANES], p[:, LANES:]
        first_out[c] = jnp.where(upper, low, high)
        first_copy[c] = send(first_out.at[c], first_in.at[c], first_sem.at[c], 0)
        keep[c] = jnp.where(upper, high, low)
        for start, n, k, both in later:
            ql_ref[c, start : start + 2 * rank] = dotk(
                [ref[k, : 2 * rank] for ref in ch_refs[n]], both
            )

    def bases():
        def turned(rows, width):
            extra = width - rank * len(rows)
            if extra:
                rows = rows + [jnp.zeros((extra, rows_dev), F32)]
            return split(-jnp.concatenate(rows, 0).T)

        if local_levels:
            high, low = turned([ut_ref[level] for level in local_levels], a_high.shape[1] - lf)
            a_high[:, lf:] = high
            a_low[:, lf:] = low
        high, low = turned([ut_ref[bits - 1 - s] for s in range(bits)], u_high.shape[1])
        u_high[...] = high
        u_low[...] = low

    def leaves(c):
        for i in range(blocks):
            rows = slice(i * lf, (i + 1) * lf)
            highs, lows = [r_high[c, rows, :]], [r_low[c, rows, :]]
            width = lf
            for level in local_levels:
                place = rank * (i * 2 ** (level - bits + 1) // blocks)
                start = local_offset(level, bits, rank) + place
                high, low = split(ql_ref[c, start : start + rank])
                highs.append(high)
                lows.append(low)
                width += rank
            if a_high.shape[1] > width:
                zero = jnp.zeros((a_high.shape[1] - width, CHUNK), BF16)
                highs.append(zero)
                lows.append(zero)
            x_ref[c, rows, :] = dotk(
                (a_high[rows, :], a_low[rows, :]),
                (jnp.concatenate(highs, 0), jnp.concatenate(lows, 0)),
            )

    def operator(s):
        core_g_loads[s].wait()
        first = child(s) == 0
        core = core_g[s]
        own = jnp.where(first, core[:rank], core[rank:])
        sib = jnp.where(first, core[rank:], core[:rank])
        parts = [own, sib] if s == 0 else [own]
        if s < bits - 1:
            gram_copy[s].wait_recv()
            rows = slice(rank * s, None)
            if s + 1 < bits - 1:
                gram_out[s + 1] = gram_out[s] + gram_in[s]
                gram_copy[s + 1] = send(
                    gram_out.at[s + 1], gram_in.at[s + 1], gram_sem.at[s + 1], s + 1
                )
            before = [jnp.zeros((rank, 2 * rank), F32)] * s
            after = [jnp.zeros((rank, 2 * rank), F32)] * (gram_cols // rank - 1 - s)
            parts.append(
                -(
                    dot(gram_out[s, rows, :], jnp.concatenate(before + [own] + after, 0))
                    + dot(gram_in[s, rows, :], jnp.concatenate(before + [sib] + after, 0))
                )
            )
        whole = jnp.concatenate(parts, 0)
        high, low = split(jnp.where(first, swap_lanes(whole), whole))
        op_high[s, : high.shape[0]] = high
        op_low[s, : low.shape[0]] = low

    def step(s, c):
        if s == 0:
            first_copy[c].wait_recv()
            mine, theirs = keep[c], first_in[c]
        else:
            later_copy[s, c].wait_recv()
            mine, theirs = later_out[s, c, rank * (s - 1) :], later_in[s, c, rank * (s - 1) :]
        count = rank * (bits - 1 - s) + (2 * rank if s == 0 else rank)
        both = split(jnp.concatenate([mine[:rank], theirs[:rank]], 0))
        image = dotk((op_high[s, :count], op_low[s, :count]), both)
        if s < bits - 1:
            later_out[s + 1, c, rank * s :] = (
                mine[rank:] + theirs[rank:] + image[count - rank * (bits - 1 - s) :]
            )
            part = pl.ds(rank * s, rank * (bits - 1 - s))
            later_copy[s + 1, c] = send(
                later_out.at[s + 1, c, part],
                later_in.at[s + 1, c, part],
                later_sem.at[s, c],
                s + 1,
            )
        q_out[s, c] = image[rank : 2 * rank] if s == 0 else image[:rank]
        q_copy[s, c] = send(
            q_out.at[s, c],
            q_all.at[c, half_id, pl.ds(rank * s, rank)],
            q_sem.at[s, c],
            0,
        )
        q_all[c, half_id, rank * s : rank * (s + 1)] = image[:rank]

    def gathered(c):
        for s in range(bits):
            q_copy[s, c].wait_recv()
        return jnp.concatenate([q_all[c, 0], q_all[c, 1]], 1)

    def apply(c):
        q = gathered(c)
        pad = u_high.shape[1] - q.shape[0]
        if pad:
            q = jnp.concatenate([q, jnp.zeros((pad, CHUNK), F32)], 0)
        x_ref[c] = x_ref[c] + dot3((u_high[...], u_low[...]), split(q))

    for c in range(chunks):
        with region(f"forward{c}"):
            forward(c)
        if c < bits:
            with region(f"operator{c}"):
                operator(c)
    for s in range(chunks, bits):
        operator(s)
    with region("bases"):
        bases()
    for name, *args in schedule(bits, chunks):
        with region(name + "_".join(str(a) for a in args)):
            {"step": step, "leaves": leaves, "apply": apply}[name](*args)
    with region("qwait"):
        q_last[...] = gathered(chunks - 1)
    with region("sent"):
        for copy in sent:
            copy.wait_send()


def tree(bits, right_side, leaf_inverse, vt, ut, cores):
    rows_dev, cols = right_side.shape
    lf = leaf_inverse.shape[1]
    levels, rank = vt.shape[:2]
    blocks = rows_dev // lf
    chunks = cols // CHUNK
    local_levels = list(range(bits, levels))
    assert blocks == 2 ** len(local_levels) and bits >= 2
    gram_cols = pl.cdiv(rank * (bits - 1), LANES) * LANES
    depth = lf + pl.cdiv(rank * len(local_levels), LANES) * LANES
    wide = pl.cdiv(rank * bits, LANES) * LANES
    out_shape = [
        jax.ShapeDtypeStruct((chunks, rows_dev, CHUNK), F32),
        jax.ShapeDtypeStruct((rank * bits, CHUNK), F32),
        jax.ShapeDtypeStruct((rows_dev, wide), BF16),
        jax.ShapeDtypeStruct((rows_dev, wide), BF16),
    ]
    hbm = pl.BlockSpec(memory_space=pltpu.HBM)
    vmem = pl.BlockSpec(memory_space=pltpu.VMEM)
    counts = [2 ** (level - bits) for level in local_levels]
    rest = rank * (bits - 1)
    scratch = [
        pltpu.VMEM((chunks, rows_dev, CHUNK), F32),
        pltpu.VMEM((rows_dev, lf), F32),
        pltpu.VMEM((levels, rank, rows_dev), F32),
        pltpu.VMEM((levels, rank, rows_dev), F32),
        pltpu.VMEM((bits, 2 * rank, 2 * rank), F32),
        pltpu.SemaphoreType.DMA((3 + levels + chunks,)),
        pltpu.VMEM((chunks, rows_dev, CHUNK), BF16),
        pltpu.VMEM((chunks, rows_dev, CHUNK), BF16),
        pltpu.VMEM((rows_dev, depth), BF16),
        pltpu.VMEM((rows_dev, depth), BF16),
        pltpu.VMEM((blocks, levels * rank, lf), BF16),
        pltpu.VMEM((blocks, levels * rank, lf), BF16),
        pltpu.VMEM((chunks, max(rank * (2 * blocks - 2), rank), CHUNK), F32),
        pltpu.VMEM((bits, rank * (bits + 1), 2 * rank), BF16),
        pltpu.VMEM((bits, rank * (bits + 1), 2 * rank), BF16),
        pltpu.VMEM((bits - 1, rest, gram_cols), F32),
        pltpu.VMEM((bits - 1, rest, gram_cols), F32),
        pltpu.VMEM((chunks, rank * bits, LANES), F32),
        pltpu.VMEM((chunks, rank * bits, LANES), F32),
        pltpu.VMEM((chunks, rank * bits, LANES), F32),
        pltpu.VMEM((bits, chunks, rest, LANES), F32),
        pltpu.VMEM((bits, chunks, rest, LANES), F32),
        pltpu.VMEM((bits, chunks, rank, LANES), F32),
        pltpu.VMEM((chunks, 2, rank * bits, LANES), F32),
        pltpu.SemaphoreType.DMA((bits - 1, 2)),
        pltpu.SemaphoreType.DMA((chunks, 2)),
        pltpu.SemaphoreType.DMA((bits - 1, chunks, 2)),
        pltpu.SemaphoreType.DMA((bits, chunks, 2)),
    ]
    scratch += [pltpu.VMEM((count, 2 * rank, 2 * rank), F32) for count in counts]
    scratch += [
        pltpu.VMEM((count, rank * (level + 2), 2 * rank), BF16)
        for count, level in zip(counts, local_levels)
        for _ in range(2)
    ]
    return pl.pallas_call(
        functools.partial(tree_kernel, bits, levels, blocks),
        out_shape=out_shape,
        in_specs=[hbm] * 5,
        out_specs=[vmem] * 4,
        scratch_shapes=scratch,
        compiler_params=pltpu.CompilerParams(
            collective_id=0, has_side_effects=True, vmem_limit_bytes=TREE_VMEM + 32 * rows_dev * lf
        ),
        name="tree",
    )(right_side, leaf_inverse, vt, ut, cores)


def finish_kernel(x_ref, q_ref, uh_ref, ul_ref, out_hbm, last, sems):
    chunks, rows_dev, width = x_ref.shape
    copies = []

    def write(src, rows, c):
        dst = out_hbm.at[pl.ds(rows, src.shape[0]), pl.ds(c * width, width)]
        copy = pltpu.make_async_copy(src, dst, sems.at[len(copies)])
        copy.start()
        copies.append(copy)

    for c in range(chunks - 1):
        write(x_ref.at[c], 0, c)
    q = q_ref[...]
    pad = uh_ref.shape[1] - q.shape[0]
    if pad:
        q = jnp.concatenate([q, jnp.zeros((pad, width), F32)], 0)
    q = split(q)
    piece = rows_dev // (sems.shape[0] - (chunks - 1))
    for start in range(0, rows_dev, piece):
        rows = slice(start, start + piece)
        last[rows] = x_ref[chunks - 1, rows] + dot3((uh_ref[rows], ul_ref[rows]), q)
        write(last.at[pl.ds(start, piece)], start, chunks - 1)
    for copy in copies:
        copy.wait()


def finish(x, q, u_high, u_low):
    chunks, rows_dev, width = x.shape
    vmem = pl.BlockSpec(memory_space=pltpu.VMEM)
    return pl.pallas_call(
        finish_kernel,
        out_shape=jax.ShapeDtypeStruct((rows_dev, chunks * width), F32),
        in_specs=[vmem] * 4,
        out_specs=pl.BlockSpec(memory_space=pltpu.HBM),
        scratch_shapes=[
            pltpu.VMEM((rows_dev, width), F32),
            pltpu.SemaphoreType.DMA((chunks - 1 + 4,)),
        ],
        compiler_params=pltpu.CompilerParams(vmem_limit_bytes=FINISH_VMEM),
        name="finish",
    )(x, q, u_high, u_low)


def local(bits, right_side, leaf_inverse, left_factors, right_factors, cores):
    ut = jnp.swapaxes(left_factors, 1, 2)
    vt = jnp.swapaxes(right_factors, 1, 2)
    right_side, leaf_inverse, vt, ut, cores = (
        pltpu.with_memory_space_constraint(a, pltpu.HBM)
        for a in (right_side, leaf_inverse, vt, ut, cores)
    )
    return finish(*tree(bits, right_side, leaf_inverse, vt, ut, cores))


def solution(mesh):
    bits = mesh.shape["rows"].bit_length() - 1
    in_specs = (
        P(("rep", "rows"), None),
        P(("rep", "rows"), None),
        P(None, ("rep", "rows"), None),
        P(None, ("rep", "rows"), None),
        P("rep", None, None),
    )
    out_specs = P(("rep", "rows"), None)
    return jax.shard_map(
        functools.partial(local, bits),
        mesh=mesh,
        in_specs=in_specs,
        out_specs=out_specs,
        check_vma=False,
    )
```

```python
import contextlib
import functools

import jax
import jax.numpy as jnp
from jax import lax
from jax.experimental import pallas as pl
from jax.experimental.pallas import tpu as pltpu
from jax.sharding import PartitionSpec as P

LANES = 128
CHUNK = 2 * LANES
F32 = jnp.float32
BF16 = jnp.bfloat16
TREE_VMEM = 24 << 20
FINISH_VMEM = 12 << 20
MESH = pl.DeviceIdType.MESH
TRACE = False
LATE = 2
PIECES = 2
CROSS = True


def region(name):
    return jax.named_scope(name) if TRACE else contextlib.nullcontext()


def split(x):
    high = x.astype(BF16)
    return high, (x - high.astype(F32)).astype(BF16)


def level_order(bits, levels):
    return [bits - 1 - s for s in range(bits)] + list(range(bits, levels))


def local_offset(level, bits, rank):
    return rank * (2 ** (level - bits + 1) - 2)


def one(x, y, nt=False):
    dims = (((1,), (1 if nt else 0,)), ((), ()))
    return lax.dot_general(x, y, dims, preferred_element_type=F32)


def dot3(a, b, nt=False):
    return one(a[0], b[0], nt) + one(a[0], b[1], nt) + one(a[1], b[0], nt)


def dotk(a, b):
    return one(
        jnp.concatenate([a[0], a[0], a[1]], 1), jnp.concatenate([b[0], b[1], b[0]], 0)
    )


def dot(a, b):
    return dotk(split(a), split(b))


def swap_lanes(x):
    half = x.shape[1] // 2
    return jnp.concatenate([x[:, half:], x[:, :half]], 1)


def schedule(bits, chunks):
    if bits == 3 and chunks == 4:
        return [
            (None, "forward", 0), (None, "forward", 1), (None, "operator", 0),
            (None, "forward", 2), (None, "step", 0, 0), (None, "forward", 3),
            (None, "give", 0, 0), (None, "step", 0, 1), (None, "bases"), (None, "operator", 1),
            (None, "step", 1, 0), (None, "give", 1, 0), (None, "step", 0, 2),
            (False, "leaves", 2), (None, "give", 0, 1), (None, "give", 0, 2),
            (None, "step", 1, 1), (False, "leaves", 0), (None, "step", 0, 3),
            (None, "operator", 2), (None, "step", 2, 0), (None, "give", 2, 0),
            (None, "give", 1, 1), (None, "step", 1, 2), (True, "leaves", 2), (None, "leaves", 1),
            (True, "leaves", 3), (True, "leaves", 0), (None, "give", 1, 2), (None, "step", 1, 3),
            (None, "step", 2, 1), (True, "apply", 0), (None, "give", 2, 1), (False, "leaves", 3),
            (None, "step", 2, 2), (None, "give", 1, 3), (None, "give", 0, 3),
            (None, "give", 2, 2), (False, "apply", 0), (None, "apply", 1), (None, "step", 2, 3),
        ]
    order = [("forward", c) for c in range(chunks)]
    order += [("operator", s) for s in range(bits)] + [("bases",)]
    for t in range(chunks + bits - 1):
        for s in range(bits):
            if 0 <= t - s < chunks:
                order.append(("step", s, t - s))
                if not (CROSS and s == bits - 1 and t - s == chunks - 1):
                    order.append(("give", s, t - s))
        if t < chunks:
            order.append(("leaves", t))
    order += [("apply", c) for c in range(chunks - LATE)]
    return [(None, *item) for item in order]


def tree_kernel(bits, levels, blocks, right_hbm, leaf_hbm, vt_hbm, ut_hbm, cores_hbm, *refs):
    x_ref, q_late, u_high, u_low = refs[:4]
    rbuf, leaf, vt_ref, ut_ref, core_g, sem_in = refs[4:10]
    r_high, r_low, a_high, a_low, m_high, m_low, ql_ref = refs[10:17]
    op_high, op_low, gram_out, gram_in, keep, first_out, first_in = refs[17:24]
    later_out, later_in, q_out, q_all = refs[24:28]
    gram_sem, first_sem, later_sem, q_sem = refs[28:32]
    last_in, last_sem = refs[32:34]
    local_levels = list(range(bits, levels))
    core_l = refs[34 : 34 + len(local_levels)]
    ch_refs = refs[34 + len(local_levels) :]
    ch_refs = list(zip(ch_refs[::2], ch_refs[1::2]))

    me = lax.axis_index("rows")
    rank, rows_dev = vt_ref.shape[1:]
    chunks = rbuf.shape[0]
    lf = rows_dev // blocks
    half_id = lax.rem(me, 2)
    upper = half_id == 1
    order = level_order(bits, levels)
    gram_cols = gram_out.shape[2]
    second = lax.rem(lax.axis_index("rep"), 2) == 1

    def child(s):
        return lax.rem(me // 2**s, 2)

    def partner(s):
        return me + (1 - 2 * child(s)) * 2**s

    cross = partner(bits - 1) + (1 - 2 * child(0))
    greeted = [partner(s) for s in range(bits)] + ([cross] if CROSS else [])
    barrier = pltpu.get_barrier_semaphore()
    for target in greeted:
        pl.semaphore_signal(barrier, inc=1, device_id={"rows": target}, device_id_type=MESH)

    slots = [0]

    def load(src, dst):
        copy = pltpu.make_async_copy(src, dst, sem_in.at[slots[0]])
        slots[0] += 1
        copy.start()
        return copy

    v_load = load(vt_hbm, vt_ref)
    leaf_load = load(leaf_hbm, leaf)
    u_load = load(ut_hbm, ut_ref)
    core_loads = []
    for n, level in enumerate(local_levels):
        count = 2 ** (level - bits)
        src = cores_hbm.at[pl.ds(2**level - 1 + me * count, count)]
        core_loads.append(load(src, core_l[n]))
    right_loads = [
        load(right_hbm.at[:, pl.ds(c * CHUNK, CHUNK)], rbuf.at[c]) for c in range(chunks)
    ]
    core_g_loads = []
    for s in range(bits):
        src = cores_hbm.at[2 ** (bits - 1 - s) - 1 + me // 2 ** (s + 1)]
        core_g_loads.append(load(src, core_g.at[s]))

    sent = []

    def send(src, dst, sems, target):
        copy = pltpu.make_async_remote_copy(
            src_ref=src,
            dst_ref=dst,
            send_sem=sems.at[0],
            recv_sem=sems.at[1],
            device_id={"rows": target},
            device_id_type=MESH,
        )
        copy.start()
        sent.append(copy)
        return copy

    with region("wait_v"):
        v_load.wait()
    vt = split(jnp.concatenate([vt_ref[level] for level in order], 0))
    with region("wait_leaf"):
        leaf_load.wait()
    with region("m"):
        high, low = split(leaf[...])
        a_high[:, :lf] = high
        a_low[:, :lf] = low
        for i in range(blocks):
            rows = slice(i * lf, (i + 1) * lf)
            high, low = split(
                dot3([v[:, rows] for v in vt], (a_high[rows, :lf], a_low[rows, :lf]))
            )
            m_high[i] = high
            m_low[i] = low
    with region("wait_u"):
        u_load.wait()
        for copy in core_loads:
            copy.wait()

    def set_local(n, k, gram):
        core = core_l[n][k]
        for ref, top, rest in zip(ch_refs[n], split(core), split(dot(gram, core))):
            ref[k, : 2 * rank] = top
            ref[k, 2 * rank :] = rest

    with region("grams"):
        fast = len(local_levels) == 2 and bits == 3 and 2 * rank == LANES
        if fast:
            ut = {level: split(ut_ref[level]) for level in range(1, levels)}
            rows_v = rank * (levels - 1)
            lane = lax.broadcasted_iota(jnp.int32, (rows_v, LANES), 1) < rank
            tile_a, tile_b = [], []
            for i in range(blocks):
                cols = slice(i * lf, (i + 1) * lf)
                names = [4, 2] if i % 2 == 0 else [2, 4]
                names += [3, 1] if i < 2 else [1, 3]
                rhs = [
                    jnp.concatenate([ut[level][j][:, cols] for level in names], 0)
                    for j in range(2)
                ]
                g = dot3([v[:rows_v, cols] for v in vt], rhs, nt=True)
                tile_a.append(g[:, :LANES])
                tile_b.append(g[:, LANES:])
            s01, s23 = tile_b[0] + tile_b[1], tile_b[2] + tile_b[3]
            even, odd = tile_a[0] + tile_a[2], tile_a[1] + tile_a[3]
            cut = slice(rank, rank * bits)
            gram_out[0] = jnp.where(
                lane[cut], odd[cut] + swap_lanes(even[cut]), s01[cut] + swap_lanes(s23[cut])
            )
        else:
            vr = [v[rank : rank * bits] for v in vt]
            ur = split(jnp.concatenate([ut_ref[level] for level in order], 0))
            gram_out[0] = dot3(vr, [u[:gram_cols] for u in ur], nt=True)
    with region("barrier"):
        pl.semaphore_wait(barrier, len(greeted))
    gram_copy = {0: send(gram_out.at[0], gram_in.at[0], gram_sem.at[0], partner(0))}
    with region("ch"):
        if fast:
            for k in range(2):
                set_local(1, k, jnp.where(lane, tile_a[2 * k], tile_a[2 * k + 1]))
            cut = slice(0, rank * bits)
            set_local(0, 0, jnp.where(lane[cut], s01[cut], s23[cut]))
        else:
            for n, level in enumerate(local_levels):
                count = 2 ** (level - bits)
                node = rows_dev // count
                half = node // 2
                zero = jnp.zeros((rank, half), BF16)
                own = slice(rank * level, rank * (level + 1))
                for k in range(count):
                    base = k * node
                    diag = [
                        jnp.concatenate(
                            [
                                jnp.concatenate([u[own, base : base + half], zero], 1),
                                jnp.concatenate([zero, u[own, base + half : base + node]], 1),
                            ],
                            0,
                        )
                        for u in ur
                    ]
                    above = [v[: rank * level, base : base + node] for v in vt]
                    set_local(n, k, dot3(above, diag, nt=True))

    first_copy, later_copy, q_copy, last_copy = {}, {}, {}, []

    def forward(c):
        right_loads[c].wait()
        high, low = split(rbuf[c])
        r_high[c] = high
        r_low[c] = low
        parts, later = [], []
        for i in range(blocks):
            rows = slice(i * lf, (i + 1) * lf)
            parts.append(dot3((m_high[i], m_low[i]), (r_high[c, rows, :], r_low[c, rows, :])))
        for n in reversed(range(len(local_levels))):
            level = local_levels[n]
            top = rank * level
            merged = []
            for k in range(len(parts) // 2):
                a, b = parts[2 * k], parts[2 * k + 1]
                both = split(jnp.concatenate([b[top:], a[top:]], 0))
                change = dotk([ref[k, 2 * rank :] for ref in ch_refs[n]], both)
                start = local_offset(level, bits, rank) + 2 * rank * k
                later.append((start, n, k, both))
                merged.append(a[:top] + b[:top] - change)
            parts = merged
        p = parts[0]
        low, high = p[:, :LANES], p[:, LANES:]
        first_out[c] = jnp.where(upper, low, high)
        first_copy[c] = send(first_out.at[c], first_in.at[c], first_sem.at[c], partner(0))
        keep[c] = jnp.where(upper, high, low)
        for start, n, k, both in later:
            ql_ref[c, start : start + 2 * rank] = dotk(
                [ref[k, : 2 * rank] for ref in ch_refs[n]], both
            )

    def bases():
        def turned(rows, width):
            extra = width - rank * len(rows)
            if extra:
                rows = rows + [jnp.zeros((extra, rows_dev), F32)]
            return split(-jnp.concatenate(rows, 0).T)

        if local_levels:
            high, low = turned([ut_ref[level] for level in local_levels], a_high.shape[1] - lf)
            a_high[:, lf:] = high
            a_low[:, lf:] = low
        high, low = turned([ut_ref[bits - 1 - s] for s in range(bits)], u_high.shape[1])
        u_high[...] = high
        u_low[...] = low

    def leaves(c):
        for i in range(blocks):
            rows = slice(i * lf, (i + 1) * lf)
            highs, lows = [r_high[c, rows, :]], [r_low[c, rows, :]]
            width = lf
            for level in local_levels:
                place = rank * (i * 2 ** (level - bits + 1) // blocks)
                start = local_offset(level, bits, rank) + place
                high, low = split(ql_ref[c, start : start + rank])
                highs.append(high)
                lows.append(low)
                width += rank
            if a_high.shape[1] > width:
                zero = jnp.zeros((a_high.shape[1] - width, CHUNK), BF16)
                highs.append(zero)
                lows.append(zero)
            x_ref[c, rows, :] = dotk(
                (a_high[rows, :], a_low[rows, :]),
                (jnp.concatenate(highs, 0), jnp.concatenate(lows, 0)),
            )

    def operator(s):
        core_g_loads[s].wait()
        first = child(s) == 0
        core = core_g[s]
        own = jnp.where(first, core[:rank], core[rank:])
        sib = jnp.where(first, core[rank:], core[:rank])
        parts = [own, sib] if s == 0 else [own]
        if s < bits - 1:
            gram_copy[s].wait_recv()
            rows = slice(rank * s, None)
            if s + 1 < bits - 1:
                gram_out[s + 1] = gram_out[s] + gram_in[s]
                gram_copy[s + 1] = send(
                    gram_out.at[s + 1],
                    gram_in.at[s + 1],
                    gram_sem.at[s + 1],
                    partner(s + 1),
                )
            before = [jnp.zeros((rank, 2 * rank), F32)] * s
            after = [jnp.zeros((rank, 2 * rank), F32)] * (gram_cols // rank - 1 - s)
            parts.append(
                -(
                    dot(gram_out[s, rows, :], jnp.concatenate(before + [own] + after, 0))
                    + dot(gram_in[s, rows, :], jnp.concatenate(before + [sib] + after, 0))
                )
            )
        whole = jnp.concatenate(parts, 0)
        high, low = split(jnp.where(first, swap_lanes(whole), whole))
        op_high[s, : high.shape[0]] = high
        op_low[s, : low.shape[0]] = low

    def crossed(s, c):
        return CROSS and s == bits - 1 and c == chunks - 1

    def halves(c, rows, value):
        q_all[c, 0, rows] = value[:, :LANES]
        q_all[c, 1, rows] = value[:, LANES:]

    def join(here, there):
        return jnp.concatenate(
            [jnp.where(upper, there, here), jnp.where(upper, here, there)], 1
        )

    def step(s, c):
        if s == 0:
            first_copy[c].wait_recv()
            mine, theirs = keep[c], first_in[c]
        else:
            later_copy[s, c].wait_recv()
            mine, theirs = later_out[s, c, rank * (s - 1) :], later_in[s, c, rank * (s - 1) :]
        if crossed(s, c):
            for copy in last_copy:
                copy.wait_recv()
            mine, theirs = join(mine, last_in[0]), join(theirs, last_in[1])
        count = rank * (bits - 1 - s) + (2 * rank if s == 0 else rank)
        both = split(jnp.concatenate([mine[:rank], theirs[:rank]], 0))
        image = dotk((op_high[s, :count], op_low[s, :count]), both)
        own = slice(rank * s, rank * (s + 1))
        if crossed(s, c):
            halves(c, own, image)
            return
        if s < bits - 1:
            later_out[s + 1, c, rank * s :] = (
                mine[rank:] + theirs[rank:] + image[count - rank * (bits - 1 - s) :]
            )
            part = pl.ds(rank * s, rank * (bits - 1 - s))
            later_copy[s + 1, c] = send(
                later_out.at[s + 1, c, part],
                later_in.at[s + 1, c, part],
                later_sem.at[s, c],
                partner(s + 1),
            )
            if crossed(s + 1, c):
                root = later_out.at[s + 1, c, pl.ds(rank * s, rank)]
                last_copy.append(send(root, last_in.at[1], last_sem.at[1], cross))
                last_copy.append(send(root, last_in.at[0], last_sem.at[0], partner(0)))
        q_out[s, c] = image[rank : 2 * rank] if s == 0 else image[:rank]
        q_all[c, half_id, own] = image[:rank]

    def give(s, c):
        q_copy[s, c] = send(
            q_out.at[s, c],
            q_all.at[c, half_id, pl.ds(rank * s, rank)],
            q_sem.at[s, c],
            partner(0),
        )

    def gathered(c):
        for s in range(bits):
            if not crossed(s, c):
                q_copy[s, c].wait_recv()
        return jnp.concatenate([q_all[c, 0], q_all[c, 1]], 1)

    def apply(c):
        q = gathered(c)
        pad = u_high.shape[1] - q.shape[0]
        if pad:
            q = jnp.concatenate([q, jnp.zeros((pad, CHUNK), F32)], 0)
        x_ref[c] = x_ref[c] + dot3((u_high[...], u_low[...]), split(q))

    parts = {f.__name__: f for f in (forward, operator, bases, step, give, leaves, apply)}
    for where, name, *args in schedule(bits, chunks):
        with region(name + "_".join(str(a) for a in args)):
            if where is None:
                parts[name](*args)
            else:
                pl.when(second == where)(functools.partial(parts[name], *args))
    with region("qwait"):
        for c in range(chunks - LATE, chunks):
            q_late[c - chunks + LATE] = gathered(c)
    with region("sent"):
        for copy in sent:
            copy.wait_send()


def tree(bits, right_side, leaf_inverse, vt, ut, cores):
    rows_dev, cols = right_side.shape
    lf = leaf_inverse.shape[1]
    levels, rank = vt.shape[:2]
    blocks = rows_dev // lf
    chunks = cols // CHUNK
    local_levels = list(range(bits, levels))
    assert blocks == 2 ** len(local_levels) and bits >= 2
    gram_cols = pl.cdiv(rank * (bits - 1), LANES) * LANES
    depth = lf + pl.cdiv(rank * len(local_levels), LANES) * LANES
    wide = pl.cdiv(rank * bits, LANES) * LANES
    out_shape = [
        jax.ShapeDtypeStruct((chunks, rows_dev, CHUNK), F32),
        jax.ShapeDtypeStruct((LATE, rank * bits, CHUNK), F32),
        jax.ShapeDtypeStruct((rows_dev, wide), BF16),
        jax.ShapeDtypeStruct((rows_dev, wide), BF16),
    ]
    hbm = pl.BlockSpec(memory_space=pltpu.HBM)
    vmem = pl.BlockSpec(memory_space=pltpu.VMEM)
    counts = [2 ** (level - bits) for level in local_levels]
    rest = rank * (bits - 1)
    scratch = [
        pltpu.VMEM((chunks, rows_dev, CHUNK), F32),
        pltpu.VMEM((rows_dev, lf), F32),
        pltpu.VMEM((levels, rank, rows_dev), F32),
        pltpu.VMEM((levels, rank, rows_dev), F32),
        pltpu.VMEM((bits, 2 * rank, 2 * rank), F32),
        pltpu.SemaphoreType.DMA((3 + levels + chunks,)),
        pltpu.VMEM((chunks, rows_dev, CHUNK), BF16),
        pltpu.VMEM((chunks, rows_dev, CHUNK), BF16),
        pltpu.VMEM((rows_dev, depth), BF16),
        pltpu.VMEM((rows_dev, depth), BF16),
        pltpu.VMEM((blocks, levels * rank, lf), BF16),
        pltpu.VMEM((blocks, levels * rank, lf), BF16),
        pltpu.VMEM((chunks, max(rank * (2 * blocks - 2), rank), CHUNK), F32),
        pltpu.VMEM((bits, rank * (bits + 1), 2 * rank), BF16),
        pltpu.VMEM((bits, rank * (bits + 1), 2 * rank), BF16),
        pltpu.VMEM((bits - 1, rest, gram_cols), F32),
        pltpu.VMEM((bits - 1, rest, gram_cols), F32),
        pltpu.VMEM((chunks, rank * bits, LANES), F32),
        pltpu.VMEM((chunks, rank * bits, LANES), F32),
        pltpu.VMEM((chunks, rank * bits, LANES), F32),
        pltpu.VMEM((bits, chunks, rest, LANES), F32),
        pltpu.VMEM((bits, chunks, rest, LANES), F32),
        pltpu.VMEM((bits, chunks, rank, LANES), F32),
        pltpu.VMEM((chunks, 2, rank * bits, LANES), F32),
        pltpu.SemaphoreType.DMA((bits - 1, 2)),
        pltpu.SemaphoreType.DMA((chunks, 2)),
        pltpu.SemaphoreType.DMA((bits - 1, chunks, 2)),
        pltpu.SemaphoreType.DMA((bits, chunks, 2)),
        pltpu.VMEM((2, rank, LANES), F32),
        pltpu.SemaphoreType.DMA((2, 2)),
    ]
    scratch += [pltpu.VMEM((count, 2 * rank, 2 * rank), F32) for count in counts]
    scratch += [
        pltpu.VMEM((count, rank * (level + 2), 2 * rank), BF16)
        for count, level in zip(counts, local_levels)
        for _ in range(2)
    ]
    return pl.pallas_call(
        functools.partial(tree_kernel, bits, levels, blocks),
        out_shape=out_shape,
        in_specs=[hbm] * 5,
        out_specs=[vmem] * 4,
        scratch_shapes=scratch,
        compiler_params=pltpu.CompilerParams(
            collective_id=0, has_side_effects=True, vmem_limit_bytes=TREE_VMEM + 32 * rows_dev * lf
        ),
        name="tree",
    )(right_side, leaf_inverse, vt, ut, cores)


def finish_kernel(x_ref, q_ref, uh_ref, ul_ref, out_hbm, last, sems):
    chunks, rows_dev, width = x_ref.shape
    copies = []

    def write(src, rows, c):
        dst = out_hbm.at[pl.ds(rows, src.shape[0]), pl.ds(c * width, width)]
        copy = pltpu.make_async_copy(src, dst, sems.at[len(copies)])
        copy.start()
        copies.append(copy)

    late = q_ref.shape[0]
    for c in range(chunks - late):
        write(x_ref.at[c], 0, c)
    piece = rows_dev // PIECES
    for n in range(late):
        q = q_ref[n]
        pad = uh_ref.shape[1] - q.shape[0]
        if pad:
            q = jnp.concatenate([q, jnp.zeros((pad, width), F32)], 0)
        q = split(q)
        c = chunks - late + n
        for start in range(0, rows_dev, piece):
            rows = slice(start, start + piece)
            last[n, rows] = x_ref[c, rows] + dot3((uh_ref[rows], ul_ref[rows]), q)
            write(last.at[n, pl.ds(start, piece)], start, c)
    for copy in copies:
        copy.wait()


def finish(x, q, u_high, u_low):
    chunks, rows_dev, width = x.shape
    vmem = pl.BlockSpec(memory_space=pltpu.VMEM)
    return pl.pallas_call(
        finish_kernel,
        out_shape=jax.ShapeDtypeStruct((rows_dev, chunks * width), F32),
        in_specs=[vmem] * 4,
        out_specs=pl.BlockSpec(memory_space=pltpu.HBM),
        scratch_shapes=[
            pltpu.VMEM((q.shape[0], rows_dev, width), F32),
            pltpu.SemaphoreType.DMA((chunks + q.shape[0] * (PIECES - 1),)),
        ],
        compiler_params=pltpu.CompilerParams(vmem_limit_bytes=FINISH_VMEM),
        name="finish",
    )(x, q, u_high, u_low)


def local(bits, right_side, leaf_inverse, left_factors, right_factors, cores):
    ut = jnp.swapaxes(left_factors, 1, 2)
    vt = jnp.swapaxes(right_factors, 1, 2)
    right_side, leaf_inverse, vt, ut, cores = (
        pltpu.with_memory_space_constraint(a, pltpu.HBM)
        for a in (right_side, leaf_inverse, vt, ut, cores)
    )
    return finish(*tree(bits, right_side, leaf_inverse, vt, ut, cores))


def solution(mesh):
    bits = mesh.shape["rows"].bit_length() - 1
    in_specs = (
        P(("rep", "rows"), None),
        P(("rep", "rows"), None),
        P(None, ("rep", "rows"), None),
        P(None, ("rep", "rows"), None),
        P("rep", None, None),
    )
    out_specs = P(("rep", "rows"), None)
    return jax.shard_map(
        functools.partial(local, bits),
        mesh=mesh,
        in_specs=in_specs,
        out_specs=out_specs,
        check_vma=False,
    )
```

```python
import contextlib
import functools

import jax
import jax.numpy as jnp
from jax import lax
from jax.experimental import pallas as pl
from jax.experimental.pallas import tpu as pltpu
from jax.sharding import PartitionSpec as P

LANES = 128
CHUNK = 2 * LANES
F32 = jnp.float32
BF16 = jnp.bfloat16
TREE_VMEM = 24 << 20
FINISH_VMEM = 12 << 20
MESH = pl.DeviceIdType.MESH
TRACE = False
LATE = 2
PIECES = 2
CROSS = True


def region(name):
    return jax.named_scope(name) if TRACE else contextlib.nullcontext()


def split(x):
    high = x.astype(BF16)
    return high, (x - high.astype(F32)).astype(BF16)


def level_order(bits, levels):
    return [bits - 1 - s for s in range(bits)] + list(range(bits, levels))


def local_offset(level, bits, rank):
    return rank * (2 ** (level - bits + 1) - 2)


def one(x, y, nt=False):
    dims = (((1,), (1 if nt else 0,)), ((), ()))
    return lax.dot_general(x, y, dims, preferred_element_type=F32)


def dot3(a, b, nt=False):
    return one(a[0], b[0], nt) + one(a[0], b[1], nt) + one(a[1], b[0], nt)


def dotk(a, b):
    return one(
        jnp.concatenate([a[0], a[0], a[1]], 1), jnp.concatenate([b[0], b[1], b[0]], 0)
    )


def dot(a, b):
    return dotk(split(a), split(b))


def swap_lanes(x):
    half = x.shape[1] // 2
    return jnp.concatenate([x[:, half:], x[:, :half]], 1)


def schedule(bits, chunks):
    if bits == 3 and chunks == 4:
        return [
            (None, "forward", 0), (None, "forward", 1), (None, "operator", 0),
            (None, "forward", 2), (None, "step", 0, 0), (None, "forward", 3),
            (None, "give", 0, 0), (None, "step", 0, 1), (None, "bases"), (None, "operator", 1),
            (None, "step", 1, 0), (None, "give", 1, 0), (None, "step", 0, 2),
            (False, "leaves", 2), (None, "give", 0, 1), (None, "give", 0, 2),
            (None, "step", 1, 1), (False, "leaves", 0), (None, "step", 0, 3),
            (None, "operator", 2), (None, "step", 2, 0), (None, "give", 2, 0),
            (None, "give", 1, 1), (None, "step", 1, 2), (True, "leaves", 2), (None, "leaves", 1),
            (True, "leaves", 3), (True, "leaves", 0), (None, "give", 1, 2), (None, "step", 1, 3),
            (None, "step", 2, 1), (True, "apply", 0), (None, "give", 2, 1), (False, "leaves", 3),
            (None, "step", 2, 2), (None, "give", 1, 3), (None, "give", 0, 3),
            (None, "give", 2, 2), (False, "apply", 0), (None, "apply", 1), (None, "step", 2, 3),
        ]
    order = [("forward", c) for c in range(chunks)]
    order += [("operator", s) for s in range(bits)] + [("bases",)]
    for t in range(chunks + bits - 1):
        for s in range(bits):
            if 0 <= t - s < chunks:
                order.append(("step", s, t - s))
                if not (CROSS and s == bits - 1 and t - s == chunks - 1):
                    order.append(("give", s, t - s))
        if t < chunks:
            order.append(("leaves", t))
    order += [("apply", c) for c in range(chunks - LATE)]
    return [(None, *item) for item in order]


def tree_kernel(bits, levels, blocks, right_hbm, leaf_hbm, vt_hbm, ut_hbm, cores_hbm, *refs):
    x_ref, q_late, u_high, u_low = refs[:4]
    rbuf, leaf, vt_ref, ut_ref, core_g, sem_in = refs[4:10]
    r_high, r_low, a_high, a_low, m_high, m_low, ql_ref = refs[10:17]
    op_high, op_low, gram_out, gram_in, keep, first_out, first_in = refs[17:24]
    later_out, later_in, q_out, q_all = refs[24:28]
    gram_sem, first_sem, later_sem, q_sem = refs[28:32]
    last_in, last_sem, send_sem = refs[32:35]
    local_levels = list(range(bits, levels))
    core_l = refs[35 : 35 + len(local_levels)]
    ch_refs = refs[35 + len(local_levels) :]
    ch_refs = list(zip(ch_refs[::2], ch_refs[1::2]))

    me = lax.axis_index("rows")
    rank, rows_dev = vt_ref.shape[1:]
    chunks = rbuf.shape[0]
    lf = rows_dev // blocks
    half_id = lax.rem(me, 2)
    upper = half_id == 1
    order = level_order(bits, levels)
    gram_cols = gram_out.shape[2]
    second = lax.rem(lax.axis_index("rep"), 2) == 1

    def child(s):
        return lax.rem(me // 2**s, 2)

    def partner(s):
        return me + (1 - 2 * child(s)) * 2**s

    cross = partner(bits - 1) + (1 - 2 * child(0))
    greeted = [partner(s) for s in range(bits)]
    barrier = pltpu.get_barrier_semaphore()
    for target in greeted:
        pl.semaphore_signal(barrier, inc=1, device_id={"rows": target}, device_id_type=MESH)

    slots = [0]

    def load(src, dst):
        copy = pltpu.make_async_copy(src, dst, sem_in.at[slots[0]])
        slots[0] += 1
        copy.start()
        return copy

    v_load = load(vt_hbm, vt_ref)
    leaf_load = load(leaf_hbm, leaf)
    u_load = load(ut_hbm, ut_ref)
    core_loads = []
    for n, level in enumerate(local_levels):
        count = 2 ** (level - bits)
        src = cores_hbm.at[pl.ds(2**level - 1 + me * count, count)]
        core_loads.append(load(src, core_l[n]))
    right_loads = [
        load(right_hbm.at[:, pl.ds(c * CHUNK, CHUNK)], rbuf.at[c]) for c in range(chunks)
    ]
    for s in range(bits):
        src = cores_hbm.at[2 ** (bits - 1 - s) - 1 + me // 2 ** (s + 1)]
        pltpu.make_async_copy(src, core_g.at[s], sem_in.at[slots[0]]).start()
    core_g_load = pltpu.make_async_copy(core_g, core_g, sem_in.at[slots[0]])

    sent = []

    def send(src, dst, sem, target):
        copy = pltpu.make_async_remote_copy(
            src_ref=src,
            dst_ref=dst,
            send_sem=send_sem.at[0],
            recv_sem=sem,
            device_id={"rows": target},
            device_id_type=MESH,
        )
        copy.start()
        sent.append(src.shape[0] * src.shape[1])
        return copy

    with region("wait_v"):
        v_load.wait()
    vt = split(jnp.concatenate([vt_ref[level] for level in order], 0))
    with region("wait_leaf"):
        leaf_load.wait()
    with region("m"):
        high, low = split(leaf[...])
        a_high[:, :lf] = high
        a_low[:, :lf] = low
        for i in range(blocks):
            rows = slice(i * lf, (i + 1) * lf)
            high, low = split(
                dot3([v[:, rows] for v in vt], (a_high[rows, :lf], a_low[rows, :lf]))
            )
            m_high[i] = high
            m_low[i] = low
    with region("wait_u"):
        u_load.wait()
        for copy in core_loads:
            copy.wait()

    def set_local(n, k, gram):
        core = core_l[n][k]
        for ref, top, rest in zip(ch_refs[n], split(core), split(dot(gram, core))):
            ref[k, : 2 * rank] = top
            ref[k, 2 * rank :] = rest

    with region("grams"):
        fast = len(local_levels) == 2 and bits == 3 and 2 * rank == LANES
        if fast:
            ut = {level: split(ut_ref[level]) for level in range(1, levels)}
            rows_v = rank * (levels - 1)
            lane = lax.broadcasted_iota(jnp.int32, (rows_v, LANES), 1) < rank
            tile_a, tile_b = [], []
            for i in range(blocks):
                cols = slice(i * lf, (i + 1) * lf)
                names = [4, 2] if i % 2 == 0 else [2, 4]
                names += [3, 1] if i < 2 else [1, 3]
                rhs = [
                    jnp.concatenate([ut[level][j][:, cols] for level in names], 0)
                    for j in range(2)
                ]
                g = dot3([v[:rows_v, cols] for v in vt], rhs, nt=True)
                tile_a.append(g[:, :LANES])
                tile_b.append(g[:, LANES:])
            s01, s23 = tile_b[0] + tile_b[1], tile_b[2] + tile_b[3]
            even, odd = tile_a[0] + tile_a[2], tile_a[1] + tile_a[3]
            cut = slice(rank, rank * bits)
            gram_out[0] = jnp.where(
                lane[cut], odd[cut] + swap_lanes(even[cut]), s01[cut] + swap_lanes(s23[cut])
            )
        else:
            vr = [v[rank : rank * bits] for v in vt]
            ur = split(jnp.concatenate([ut_ref[level] for level in order], 0))
            gram_out[0] = dot3(vr, [u[:gram_cols] for u in ur], nt=True)
    with region("barrier"):
        pl.semaphore_wait(barrier, len(greeted))
    gram_copy = {0: send(gram_out.at[0], gram_in.at[0], gram_sem.at[0], partner(0))}
    with region("ch"):
        if fast:
            for k in range(2):
                set_local(1, k, jnp.where(lane, tile_a[2 * k], tile_a[2 * k + 1]))
            cut = slice(0, rank * bits)
            set_local(0, 0, jnp.where(lane[cut], s01[cut], s23[cut]))
        else:
            for n, level in enumerate(local_levels):
                count = 2 ** (level - bits)
                node = rows_dev // count
                half = node // 2
                zero = jnp.zeros((rank, half), BF16)
                own = slice(rank * level, rank * (level + 1))
                for k in range(count):
                    base = k * node
                    diag = [
                        jnp.concatenate(
                            [
                                jnp.concatenate([u[own, base : base + half], zero], 1),
                                jnp.concatenate([zero, u[own, base + half : base + node]], 1),
                            ],
                            0,
                        )
                        for u in ur
                    ]
                    above = [v[: rank * level, base : base + node] for v in vt]
                    set_local(n, k, dot3(above, diag, nt=True))

    first_copy, later_copy, last_copy = {}, {}, []

    def forward(c):
        right_loads[c].wait()
        high, low = split(rbuf[c])
        r_high[c] = high
        r_low[c] = low
        parts, later = [], []
        for i in range(blocks):
            rows = slice(i * lf, (i + 1) * lf)
            parts.append(dot3((m_high[i], m_low[i]), (r_high[c, rows, :], r_low[c, rows, :])))
        for n in reversed(range(len(local_levels))):
            level = local_levels[n]
            top = rank * level
            merged = []
            for k in range(len(parts) // 2):
                a, b = parts[2 * k], parts[2 * k + 1]
                both = split(jnp.concatenate([b[top:], a[top:]], 0))
                change = dotk([ref[k, 2 * rank :] for ref in ch_refs[n]], both)
                start = local_offset(level, bits, rank) + 2 * rank * k
                later.append((start, n, k, both))
                merged.append(a[:top] + b[:top] - change)
            parts = merged
        p = parts[0]
        low, high = p[:, :LANES], p[:, LANES:]
        first_out[c] = jnp.where(upper, low, high)
        first_copy[c] = send(first_out.at[c], first_in.at[c], first_sem.at[c], partner(0))
        keep[c] = jnp.where(upper, high, low)
        for start, n, k, both in later:
            ql_ref[c, start : start + 2 * rank] = dotk(
                [ref[k, : 2 * rank] for ref in ch_refs[n]], both
            )

    def bases():
        def turned(rows, width):
            extra = width - rank * len(rows)
            if extra:
                rows = rows + [jnp.zeros((extra, rows_dev), F32)]
            return split(-jnp.concatenate(rows, 0).T)

        if local_levels:
            high, low = turned([ut_ref[level] for level in local_levels], a_high.shape[1] - lf)
            a_high[:, lf:] = high
            a_low[:, lf:] = low
        high, low = turned([ut_ref[bits - 1 - s] for s in range(bits)], u_high.shape[1])
        u_high[...] = high
        u_low[...] = low

    def leaves(c):
        for i in range(blocks):
            rows = slice(i * lf, (i + 1) * lf)
            highs, lows = [r_high[c, rows, :]], [r_low[c, rows, :]]
            width = lf
            for level in local_levels:
                place = rank * (i * 2 ** (level - bits + 1) // blocks)
                start = local_offset(level, bits, rank) + place
                high, low = split(ql_ref[c, start : start + rank])
                highs.append(high)
                lows.append(low)
                width += rank
            if a_high.shape[1] > width:
                zero = jnp.zeros((a_high.shape[1] - width, CHUNK), BF16)
                highs.append(zero)
                lows.append(zero)
            x_ref[c, rows, :] = dotk(
                (a_high[rows, :], a_low[rows, :]),
                (jnp.concatenate(highs, 0), jnp.concatenate(lows, 0)),
            )

    def operator(s):
        if s == 0:
            core_g_load.wait()
        first = child(s) == 0
        core = core_g[s]
        own = jnp.where(first, core[:rank], core[rank:])
        sib = jnp.where(first, core[rank:], core[:rank])
        parts = [own, sib] if s == 0 else [own]
        if s < bits - 1:
            gram_copy[s].wait_recv()
            rows = slice(rank * s, None)
            if s + 1 < bits - 1:
                gram_out[s + 1] = gram_out[s] + gram_in[s]
                gram_copy[s + 1] = send(
                    gram_out.at[s + 1],
                    gram_in.at[s + 1],
                    gram_sem.at[s + 1],
                    partner(s + 1),
                )
            before = [jnp.zeros((rank, 2 * rank), F32)] * s
            after = [jnp.zeros((rank, 2 * rank), F32)] * (gram_cols // rank - 1 - s)
            parts.append(
                -(
                    dot(gram_out[s, rows, :], jnp.concatenate(before + [own] + after, 0))
                    + dot(gram_in[s, rows, :], jnp.concatenate(before + [sib] + after, 0))
                )
            )
        whole = jnp.concatenate(parts, 0)
        high, low = split(jnp.where(first, swap_lanes(whole), whole))
        op_high[s, : high.shape[0]] = high
        op_low[s, : low.shape[0]] = low

    def crossed(s, c):
        return CROSS and s == bits - 1 and c == chunks - 1

    def halves(c, rows, value):
        q_all[c, 0, rows] = value[:, :LANES]
        q_all[c, 1, rows] = value[:, LANES:]

    def join(here, there):
        return jnp.concatenate(
            [jnp.where(upper, there, here), jnp.where(upper, here, there)], 1
        )

    def step(s, c):
        if s == 0:
            first_copy[c].wait_recv()
            mine, theirs = keep[c], first_in[c]
        else:
            later_copy[s, c].wait_recv()
            mine, theirs = later_out[s, c, rank * (s - 1) :], later_in[s, c, rank * (s - 1) :]
        if crossed(s, c):
            for copy in last_copy:
                copy.wait_recv()
            mine, theirs = join(mine, last_in[0]), join(theirs, last_in[1])
        count = rank * (bits - 1 - s) + (2 * rank if s == 0 else rank)
        both = split(jnp.concatenate([mine[:rank], theirs[:rank]], 0))
        image = dotk((op_high[s, :count], op_low[s, :count]), both)
        own = slice(rank * s, rank * (s + 1))
        if crossed(s, c):
            halves(c, own, image)
            return
        if s < bits - 1:
            later_out[s + 1, c, rank * s :] = (
                mine[rank:] + theirs[rank:] + image[count - rank * (bits - 1 - s) :]
            )
            part = pl.ds(rank * s, rank * (bits - 1 - s))
            later_copy[s + 1, c] = send(
                later_out.at[s + 1, c, part],
                later_in.at[s + 1, c, part],
                later_sem.at[s, c],
                partner(s + 1),
            )
            if crossed(s + 1, c):
                root = later_out.at[s + 1, c, pl.ds(rank * s, rank)]
                last_copy.append(send(root, last_in.at[1], last_sem.at[1], cross))
                last_copy.append(send(root, last_in.at[0], last_sem.at[0], partner(0)))
        q_out[s, c] = image[rank : 2 * rank] if s == 0 else image[:rank]
        q_all[c, half_id, own] = image[:rank]

    def give(s, c):
        place = q_all.at[c, half_id, pl.ds(rank * s, rank)]
        send(q_out.at[s, c], place, q_sem.at[c], partner(0))

    def gathered(c):
        given = q_all.at[c, 0, pl.ds(0, rank * (bits - 1 if crossed(bits - 1, c) else bits))]
        pltpu.make_async_copy(given, given, q_sem.at[c]).wait()
        return jnp.concatenate([q_all[c, 0], q_all[c, 1]], 1)

    def apply(c):
        q = gathered(c)
        pad = u_high.shape[1] - q.shape[0]
        if pad:
            q = jnp.concatenate([q, jnp.zeros((pad, CHUNK), F32)], 0)
        x_ref[c] = x_ref[c] + dot3((u_high[...], u_low[...]), split(q))

    parts = {f.__name__: f for f in (forward, operator, bases, step, give, leaves, apply)}
    for where, name, *args in schedule(bits, chunks):
        with region(name + "_".join(str(a) for a in args)):
            if where is None:
                parts[name](*args)
            else:
                pl.when(second == where)(functools.partial(parts[name], *args))
    with region("qwait"):
        for c in range(chunks - LATE, chunks):
            q_late[c - chunks + LATE] = gathered(c)
    with region("sent"):
        rows = sum(sent) // (chunks * CHUNK)
        assert rows * chunks * CHUNK == sum(sent) and rows <= rows_dev
        everything = rbuf.at[:, pl.ds(0, rows)]
        pltpu.make_async_copy(everything, everything, send_sem.at[0]).wait()


def tree(bits, right_side, leaf_inverse, vt, ut, cores):
    rows_dev, cols = right_side.shape
    lf = leaf_inverse.shape[1]
    levels, rank = vt.shape[:2]
    blocks = rows_dev // lf
    chunks = cols // CHUNK
    local_levels = list(range(bits, levels))
    assert blocks == 2 ** len(local_levels) and bits >= 2
    gram_cols = pl.cdiv(rank * (bits - 1), LANES) * LANES
    depth = lf + pl.cdiv(rank * len(local_levels), LANES) * LANES
    wide = pl.cdiv(rank * bits, LANES) * LANES
    out_shape = [
        jax.ShapeDtypeStruct((chunks, rows_dev, CHUNK), F32),
        jax.ShapeDtypeStruct((LATE, rank * bits, CHUNK), F32),
        jax.ShapeDtypeStruct((rows_dev, wide), BF16),
        jax.ShapeDtypeStruct((rows_dev, wide), BF16),
    ]
    hbm = pl.BlockSpec(memory_space=pltpu.HBM)
    vmem = pl.BlockSpec(memory_space=pltpu.VMEM)
    counts = [2 ** (level - bits) for level in local_levels]
    rest = rank * (bits - 1)
    scratch = [
        pltpu.VMEM((chunks, rows_dev, CHUNK), F32),
        pltpu.VMEM((rows_dev, lf), F32),
        pltpu.VMEM((levels, rank, rows_dev), F32),
        pltpu.VMEM((levels, rank, rows_dev), F32),
        pltpu.VMEM((bits, 2 * rank, 2 * rank), F32),
        pltpu.SemaphoreType.DMA((4 + len(local_levels) + chunks,)),
        pltpu.VMEM((chunks, rows_dev, CHUNK), BF16),
        pltpu.VMEM((chunks, rows_dev, CHUNK), BF16),
        pltpu.VMEM((rows_dev, depth), BF16),
        pltpu.VMEM((rows_dev, depth), BF16),
        pltpu.VMEM((blocks, levels * rank, lf), BF16),
        pltpu.VMEM((blocks, levels * rank, lf), BF16),
        pltpu.VMEM((chunks, max(rank * (2 * blocks - 2), rank), CHUNK), F32),
        pltpu.VMEM((bits, rank * (bits + 1), 2 * rank), BF16),
        pltpu.VMEM((bits, rank * (bits + 1), 2 * rank), BF16),
        pltpu.VMEM((bits - 1, rest, gram_cols), F32),
        pltpu.VMEM((bits - 1, rest, gram_cols), F32),
        pltpu.VMEM((chunks, rank * bits, LANES), F32),
        pltpu.VMEM((chunks, rank * bits, LANES), F32),
        pltpu.VMEM((chunks, rank * bits, LANES), F32),
        pltpu.VMEM((bits, chunks, rest, LANES), F32),
        pltpu.VMEM((bits, chunks, rest, LANES), F32),
        pltpu.VMEM((bits, chunks, rank, LANES), F32),
        pltpu.VMEM((chunks, 2, rank * bits, LANES), F32),
        pltpu.SemaphoreType.DMA((bits - 1,)),
        pltpu.SemaphoreType.DMA((chunks,)),
        pltpu.SemaphoreType.DMA((bits - 1, chunks)),
        pltpu.SemaphoreType.DMA((chunks,)),
        pltpu.VMEM((2, rank, LANES), F32),
        pltpu.SemaphoreType.DMA((2,)),
        pltpu.SemaphoreType.DMA((1,)),
    ]
    scratch += [pltpu.VMEM((count, 2 * rank, 2 * rank), F32) for count in counts]
    scratch += [
        pltpu.VMEM((count, rank * (level + 2), 2 * rank), BF16)
        for count, level in zip(counts, local_levels)
        for _ in range(2)
    ]
    return pl.pallas_call(
        functools.partial(tree_kernel, bits, levels, blocks),
        out_shape=out_shape,
        in_specs=[hbm] * 5,
        out_specs=[vmem] * 4,
        scratch_shapes=scratch,
        compiler_params=pltpu.CompilerParams(
            collective_id=0, has_side_effects=True, vmem_limit_bytes=TREE_VMEM + 32 * rows_dev * lf
        ),
        name="tree",
    )(right_side, leaf_inverse, vt, ut, cores)


def finish_kernel(x_ref, q_ref, uh_ref, ul_ref, out_hbm, last, sems):
    chunks, rows_dev, width = x_ref.shape
    copies = []

    def write(src, rows, c):
        dst = out_hbm.at[pl.ds(rows, src.shape[0]), pl.ds(c * width, width)]
        copy = pltpu.make_async_copy(src, dst, sems.at[len(copies)])
        copy.start()
        copies.append(copy)

    late = q_ref.shape[0]
    for c in range(chunks - late):
        write(x_ref.at[c], 0, c)
    piece = rows_dev // PIECES
    for n in range(late):
        q = q_ref[n]
        pad = uh_ref.shape[1] - q.shape[0]
        if pad:
            q = jnp.concatenate([q, jnp.zeros((pad, width), F32)], 0)
        q = split(q)
        c = chunks - late + n
        for start in range(0, rows_dev, piece):
            rows = slice(start, start + piece)
            last[n, rows] = x_ref[c, rows] + dot3((uh_ref[rows], ul_ref[rows]), q)
            write(last.at[n, pl.ds(start, piece)], start, c)
    for copy in copies:
        copy.wait()


def finish(x, q, u_high, u_low):
    chunks, rows_dev, width = x.shape
    vmem = pl.BlockSpec(memory_space=pltpu.VMEM)
    return pl.pallas_call(
        finish_kernel,
        out_shape=jax.ShapeDtypeStruct((rows_dev, chunks * width), F32),
        in_specs=[vmem] * 4,
        out_specs=pl.BlockSpec(memory_space=pltpu.HBM),
        scratch_shapes=[
            pltpu.VMEM((q.shape[0], rows_dev, width), F32),
            pltpu.SemaphoreType.DMA((chunks + q.shape[0] * (PIECES - 1),)),
        ],
        compiler_params=pltpu.CompilerParams(vmem_limit_bytes=FINISH_VMEM),
        name="finish",
    )(x, q, u_high, u_low)


def local(bits, right_side, leaf_inverse, left_factors, right_factors, cores):
    ut = jnp.swapaxes(left_factors, 1, 2)
    vt = jnp.swapaxes(right_factors, 1, 2)
    right_side, leaf_inverse, vt, ut, cores = (
        pltpu.with_memory_space_constraint(a, pltpu.HBM)
        for a in (right_side, leaf_inverse, vt, ut, cores)
    )
    return finish(*tree(bits, right_side, leaf_inverse, vt, ut, cores))


def solution(mesh):
    bits = mesh.shape["rows"].bit_length() - 1
    in_specs = (
        P(("rep", "rows"), None),
        P(("rep", "rows"), None),
        P(None, ("rep", "rows"), None),
        P(None, ("rep", "rows"), None),
        P("rep", None, None),
    )
    out_specs = P(("rep", "rows"), None)
    return jax.shard_map(
        functools.partial(local, bits),
        mesh=mesh,
        in_specs=in_specs,
        out_specs=out_specs,
        check_vma=False,
    )
```

```python
import contextlib
import functools

import jax
import jax.numpy as jnp
from jax import lax
from jax.experimental import pallas as pl
from jax.experimental.pallas import tpu as pltpu
from jax.sharding import PartitionSpec as P

LANES = 128
CHUNK = 2 * LANES
F32 = jnp.float32
BF16 = jnp.bfloat16
TREE_VMEM = 24 << 20
FINISH_VMEM = 12 << 20
MESH = pl.DeviceIdType.MESH
TRACE = False
LATE = 2
PIECES = 2
CROSS = True


def region(name):
    return jax.named_scope(name) if TRACE else contextlib.nullcontext()


def split(x):
    high = x.astype(BF16)
    return high, (x - high.astype(F32)).astype(BF16)


def level_order(bits, levels):
    return [bits - 1 - s for s in range(bits)] + list(range(bits, levels))


def local_offset(level, bits, rank):
    return rank * (2 ** (level - bits + 1) - 2)


def one(x, y, nt=False):
    dims = (((1,), (1 if nt else 0,)), ((), ()))
    return lax.dot_general(x, y, dims, preferred_element_type=F32)


def dot3(a, b, nt=False):
    return one(a[0], b[0], nt) + one(a[0], b[1], nt) + one(a[1], b[0], nt)


def dotk(a, b):
    return one(
        jnp.concatenate([a[0], a[0], a[1]], 1), jnp.concatenate([b[0], b[1], b[0]], 0)
    )


def dot(a, b):
    return dotk(split(a), split(b))


def swap_lanes(x):
    half = x.shape[1] // 2
    return jnp.concatenate([x[:, half:], x[:, :half]], 1)


def schedule(bits, chunks):
    if bits == 3 and chunks == 4:
        return [
            (None, "forward", 0), (True, "bases"), (None, "forward", 1), (None, "operator", 0),
            (True, "leaves", 0), (None, "forward", 2), (None, "step", 0, 0), (None, "forward", 3),
            (None, "step", 0, 1), (None, "operator", 1), (False, "bases"), (None, "step", 1, 0),
            (None, "step", 0, 2), (False, "leaves", 3), (None, "step", 0, 3),
            (None, "give", 0, 0), (None, "give", 1, 0), (None, "give", 0, 1),
            (None, "step", 1, 1), (True, "leaves", 3), (False, "leaves", 2), (None, "give", 0, 2),
            (None, "give", 0, 3), (None, "give", 1, 1), (None, "operator", 2),
            (None, "step", 1, 2), (None, "give", 1, 2), (None, "step", 2, 0),
            (None, "give", 2, 0), (True, "leaves", 2), (False, "leaves", 1), (None, "step", 1, 3),
            (True, "leaves", 1), (False, "leaves", 0), (None, "step", 2, 1), (None, "give", 1, 3),
            (None, "give", 2, 1), ("early", "apply", 0), (None, "step", 2, 2),
            (None, "give", 2, 2), ("late", "apply", 0), (None, "apply", 1), (None, "step", 2, 3),
        ]
    order = [("forward", c) for c in range(chunks)]
    order += [("operator", s) for s in range(bits)] + [("bases",)]
    for t in range(chunks + bits - 1):
        for s in range(bits):
            if 0 <= t - s < chunks:
                order.append(("step", s, t - s))
                if not (CROSS and s == bits - 1 and t - s == chunks - 1):
                    order.append(("give", s, t - s))
        if t < chunks:
            order.append(("leaves", t))
    order += [("apply", c) for c in range(chunks - LATE)]
    return [(None, *item) for item in order]


def tree_kernel(bits, levels, blocks, right_hbm, leaf_hbm, vt_hbm, ut_hbm, cores_hbm, *refs):
    x_ref, q_late, u_high, u_low = refs[:4]
    rbuf, leaf, vt_ref, ut_ref, core_g, sem_in = refs[4:10]
    r_high, r_low, a_high, a_low, m_high, m_low, *both_refs = refs[10:18]
    op_high, op_low, gram_out, gram_in, keep, first_out, first_in = refs[18:25]
    later_out, later_in, q_out, q_all = refs[25:29]
    gram_sem, first_sem, later_sem, q_sem = refs[29:33]
    last_in, last_sem, send_sem = refs[33:36]
    local_levels = list(range(bits, levels))
    core_l = refs[36 : 36 + len(local_levels)]
    ch_refs = refs[36 + len(local_levels) :]
    ch_refs = list(zip(ch_refs[::2], ch_refs[1::2]))

    me = lax.axis_index("rows")
    rank, rows_dev = vt_ref.shape[1:]
    chunks = rbuf.shape[0]
    lf = rows_dev // blocks
    half_id = lax.rem(me, 2)
    upper = half_id == 1
    order = level_order(bits, levels)
    gram_cols = gram_out.shape[2]
    second = lax.rem(lax.axis_index("rep"), 2) == 1

    def child(s):
        return lax.rem(me // 2**s, 2)

    def partner(s):
        return me + (1 - 2 * child(s)) * 2**s

    cross = partner(bits - 1) + (1 - 2 * child(0))
    greeted = [partner(s) for s in range(bits)]
    barrier = pltpu.get_barrier_semaphore()
    for target in greeted:
        pl.semaphore_signal(barrier, inc=1, device_id={"rows": target}, device_id_type=MESH)

    slots = [0]

    def load(src, dst):
        copy = pltpu.make_async_copy(src, dst, sem_in.at[slots[0]])
        slots[0] += 1
        copy.start()
        return copy

    pieces = 2 if blocks % 2 == 0 else 1
    width = rows_dev // pieces
    v_loads, leaf_loads = [], []
    for n in range(pieces):
        part = pl.ds(n * width, width)
        v_loads.append(load(vt_hbm.at[:, :, part], vt_ref.at[:, :, part]))
        leaf_loads.append(load(leaf_hbm.at[part], leaf.at[part]))
    u_load = load(ut_hbm, ut_ref)
    core_loads = []
    for n, level in enumerate(local_levels):
        count = 2 ** (level - bits)
        src = cores_hbm.at[pl.ds(2**level - 1 + me * count, count)]
        core_loads.append(load(src, core_l[n]))
    right_loads = [
        load(right_hbm.at[:, pl.ds(c * CHUNK, CHUNK)], rbuf.at[c]) for c in range(chunks)
    ]
    for s in range(bits):
        src = cores_hbm.at[2 ** (bits - 1 - s) - 1 + me // 2 ** (s + 1)]
        pltpu.make_async_copy(src, core_g.at[s], sem_in.at[slots[0]]).start()
    core_g_load = pltpu.make_async_copy(core_g, core_g, sem_in.at[slots[0]])

    sent = []

    def send(src, dst, sem, target):
        copy = pltpu.make_async_remote_copy(
            src_ref=src,
            dst_ref=dst,
            send_sem=send_sem.at[0],
            recv_sem=sem,
            device_id={"rows": target},
            device_id_type=MESH,
        )
        copy.start()
        sent.append(src.shape[0] * src.shape[1])
        return copy

    vt = []
    for n in range(pieces):
        part = slice(n * width, (n + 1) * width)
        with region(f"wait_v{n}"):
            v_loads[n].wait()
        v = split(jnp.concatenate([vt_ref[level, :, part] for level in order], 0))
        vt.append(v)
        with region(f"wait_leaf{n}"):
            leaf_loads[n].wait()
        with region(f"m{n}"):
            high, low = split(leaf[part])
            a_high[part, :lf] = high
            a_low[part, :lf] = low
            for i in range(n * blocks // pieces, (n + 1) * blocks // pieces):
                rows = slice(i * lf, (i + 1) * lf)
                cols = slice(i * lf - n * width, (i + 1) * lf - n * width)
                high, low = split(dot3([x[:, cols] for x in v], (a_high[rows, :lf], a_low[rows, :lf])))
                m_high[i] = high
                m_low[i] = low
    vt = [jnp.concatenate(x, 1) for x in zip(*vt)]
    with region("wait_u"):
        u_load.wait()
        for copy in core_loads:
            copy.wait()

    def set_local(n, k, gram):
        core = core_l[n][k]
        for ref, top, rest in zip(ch_refs[n], split(core), split(dot(gram, core))):
            ref[k, : 2 * rank] = top
            ref[k, 2 * rank :] = rest

    with region("grams"):
        fast = len(local_levels) == 2 and bits == 3 and 2 * rank == LANES
        if fast:
            ut = {level: split(ut_ref[level]) for level in range(1, levels)}
            rows_v = rank * (levels - 1)
            lane = lax.broadcasted_iota(jnp.int32, (rows_v, LANES), 1) < rank
            tile_a, tile_b = [], []
            for i in range(blocks):
                cols = slice(i * lf, (i + 1) * lf)
                names = [4, 2] if i % 2 == 0 else [2, 4]
                names += [3, 1] if i < 2 else [1, 3]
                rhs = [
                    jnp.concatenate([ut[level][j][:, cols] for level in names], 0)
                    for j in range(2)
                ]
                g = dot3([v[:rows_v, cols] for v in vt], rhs, nt=True)
                tile_a.append(g[:, :LANES])
                tile_b.append(g[:, LANES:])
            s01, s23 = tile_b[0] + tile_b[1], tile_b[2] + tile_b[3]
            even, odd = tile_a[0] + tile_a[2], tile_a[1] + tile_a[3]
            cut = slice(rank, rank * bits)
            gram_out[0] = jnp.where(
                lane[cut], odd[cut] + swap_lanes(even[cut]), s01[cut] + swap_lanes(s23[cut])
            )
        else:
            vr = [v[rank : rank * bits] for v in vt]
            ur = split(jnp.concatenate([ut_ref[level] for level in order], 0))
            gram_out[0] = dot3(vr, [u[:gram_cols] for u in ur], nt=True)
    with region("barrier"):
        pl.semaphore_wait(barrier, len(greeted))
    gram_copy = {0: send(gram_out.at[0], gram_in.at[0], gram_sem.at[0], partner(0))}
    with region("ch"):
        if fast:
            for k in range(2):
                set_local(1, k, jnp.where(lane, tile_a[2 * k], tile_a[2 * k + 1]))
            cut = slice(0, rank * bits)
            set_local(0, 0, jnp.where(lane[cut], s01[cut], s23[cut]))
        else:
            for n, level in enumerate(local_levels):
                count = 2 ** (level - bits)
                node = rows_dev // count
                half = node // 2
                zero = jnp.zeros((rank, half), BF16)
                own = slice(rank * level, rank * (level + 1))
                for k in range(count):
                    base = k * node
                    diag = [
                        jnp.concatenate(
                            [
                                jnp.concatenate([u[own, base : base + half], zero], 1),
                                jnp.concatenate([zero, u[own, base + half : base + node]], 1),
                            ],
                            0,
                        )
                        for u in ur
                    ]
                    above = [v[: rank * level, base : base + node] for v in vt]
                    set_local(n, k, dot3(above, diag, nt=True))

    first_copy, later_copy, last_copy = {}, {}, []

    def forward(c):
        right_loads[c].wait()
        high, low = split(rbuf[c])
        r_high[c] = high
        r_low[c] = low
        parts = []
        for i in range(blocks):
            rows = slice(i * lf, (i + 1) * lf)
            parts.append(dot3((m_high[i], m_low[i]), (r_high[c, rows, :], r_low[c, rows, :])))
        for n in reversed(range(len(local_levels))):
            level = local_levels[n]
            top = rank * level
            merged = []
            for k in range(len(parts) // 2):
                a, b = parts[2 * k], parts[2 * k + 1]
                both = split(jnp.concatenate([b[top:], a[top:]], 0))
                change = dotk([ref[k, 2 * rank :] for ref in ch_refs[n]], both)
                start = local_offset(level, bits, rank) + 2 * rank * k
                for ref, value in zip(both_refs, both):
                    ref[c, start : start + 2 * rank] = value
                merged.append(a[:top] + b[:top] - change)
            parts = merged
        p = parts[0]
        low, high = p[:, :LANES], p[:, LANES:]
        first_out[c] = jnp.where(upper, low, high)
        first_copy[c] = send(first_out.at[c], first_in.at[c], first_sem.at[c], partner(0))
        keep[c] = jnp.where(upper, high, low)

    def bases():
        def turned(rows, width):
            extra = width - rank * len(rows)
            if extra:
                rows = rows + [jnp.zeros((extra, rows_dev), F32)]
            return split(-jnp.concatenate(rows, 0).T)

        if local_levels:
            high, low = turned([ut_ref[level] for level in local_levels], a_high.shape[1] - lf)
            a_high[:, lf:] = high
            a_low[:, lf:] = low
        high, low = turned([ut_ref[bits - 1 - s] for s in range(bits)], u_high.shape[1])
        u_high[...] = high
        u_low[...] = low

    def leaves(c):
        images = []
        for n, level in enumerate(local_levels):
            for k in range(2 ** (level - bits)):
                start = local_offset(level, bits, rank) + 2 * rank * k
                both = [ref[c, start : start + 2 * rank] for ref in both_refs]
                images.append(split(dotk([ref[k, : 2 * rank] for ref in ch_refs[n]], both)))
        for i in range(blocks):
            rows = slice(i * lf, (i + 1) * lf)
            highs, lows = [r_high[c, rows, :]], [r_low[c, rows, :]]
            width = lf
            for level in local_levels:
                place = rank * (i * 2 ** (level - bits + 1) // blocks)
                start = local_offset(level, bits, rank) + place
                high, low = images[start // (2 * rank)]
                part = slice(start % (2 * rank), start % (2 * rank) + rank)
                highs.append(high[part])
                lows.append(low[part])
                width += rank
            if a_high.shape[1] > width:
                zero = jnp.zeros((a_high.shape[1] - width, CHUNK), BF16)
                highs.append(zero)
                lows.append(zero)
            x_ref[c, rows, :] = dotk(
                (a_high[rows, :], a_low[rows, :]),
                (jnp.concatenate(highs, 0), jnp.concatenate(lows, 0)),
            )

    def operator(s):
        if s == 0:
            core_g_load.wait()
        first = child(s) == 0
        core = core_g[s]
        own = jnp.where(first, core[:rank], core[rank:])
        sib = jnp.where(first, core[rank:], core[:rank])
        parts = [own, sib] if s == 0 else [own]
        if s < bits - 1:
            gram_copy[s].wait_recv()
            rows = slice(rank * s, None)
            if s + 1 < bits - 1:
                gram_out[s + 1] = gram_out[s] + gram_in[s]
                gram_copy[s + 1] = send(
                    gram_out.at[s + 1],
                    gram_in.at[s + 1],
                    gram_sem.at[s + 1],
                    partner(s + 1),
                )
            before = [jnp.zeros((rank, 2 * rank), F32)] * s
            after = [jnp.zeros((rank, 2 * rank), F32)] * (gram_cols // rank - 1 - s)
            parts.append(
                -(
                    dot(gram_out[s, rows, :], jnp.concatenate(before + [own] + after, 0))
                    + dot(gram_in[s, rows, :], jnp.concatenate(before + [sib] + after, 0))
                )
            )
        whole = jnp.concatenate(parts, 0)
        high, low = split(jnp.where(first, swap_lanes(whole), whole))
        op_high[s, : high.shape[0]] = high
        op_low[s, : low.shape[0]] = low

    def crossed(s, c):
        return CROSS and s == bits - 1 and c == chunks - 1

    def halves(c, rows, value):
        q_all[c, 0, rows] = value[:, :LANES]
        q_all[c, 1, rows] = value[:, LANES:]

    def join(here, there):
        return jnp.concatenate(
            [jnp.where(upper, there, here), jnp.where(upper, here, there)], 1
        )

    def step(s, c):
        if s == 0:
            first_copy[c].wait_recv()
            mine, theirs = keep[c], first_in[c]
        else:
            later_copy[s, c].wait_recv()
            mine, theirs = later_out[s, c, rank * (s - 1) :], later_in[s, c, rank * (s - 1) :]
        if crossed(s, c):
            for copy in last_copy:
                copy.wait_recv()
            mine, theirs = join(mine, last_in[0]), join(theirs, last_in[1])
        count = rank * (bits - 1 - s) + (2 * rank if s == 0 else rank)
        both = split(jnp.concatenate([mine[:rank], theirs[:rank]], 0))
        image = dotk((op_high[s, :count], op_low[s, :count]), both)
        own = slice(rank * s, rank * (s + 1))
        if crossed(s, c):
            halves(c, own, image)
            return
        if s < bits - 1:
            later_out[s + 1, c, rank * s :] = (
                mine[rank:] + theirs[rank:] + image[count - rank * (bits - 1 - s) :]
            )
            part = pl.ds(rank * s, rank * (bits - 1 - s))
            later_copy[s + 1, c] = send(
                later_out.at[s + 1, c, part],
                later_in.at[s + 1, c, part],
                later_sem.at[s, c],
                partner(s + 1),
            )
            if crossed(s + 1, c):
                root = later_out.at[s + 1, c, pl.ds(rank * s, rank)]
                last_copy.append(send(root, last_in.at[1], last_sem.at[1], cross))
                last_copy.append(send(root, last_in.at[0], last_sem.at[0], partner(0)))
        q_out[s, c] = image[rank : 2 * rank] if s == 0 else image[:rank]
        q_all[c, half_id, own] = image[:rank]

    def give(s, c):
        place = q_all.at[c, half_id, pl.ds(rank * s, rank)]
        send(q_out.at[s, c], place, q_sem.at[c], partner(0))

    def gathered(c):
        given = q_all.at[c, 0, pl.ds(0, rank * (bits - 1 if crossed(bits - 1, c) else bits))]
        pltpu.make_async_copy(given, given, q_sem.at[c]).wait()
        return jnp.concatenate([q_all[c, 0], q_all[c, 1]], 1)

    def apply(c):
        q = gathered(c)
        pad = u_high.shape[1] - q.shape[0]
        if pad:
            q = jnp.concatenate([q, jnp.zeros((pad, CHUNK), F32)], 0)
        x_ref[c] = x_ref[c] + dot3((u_high[...], u_low[...]), split(q))

    parts = {f.__name__: f for f in (forward, operator, bases, step, give, leaves, apply)}
    early = (child(bits - 1) == 0) & (child(0) == 0)
    groups = {True: second, False: ~second, "late": ~early, "early": early}
    for where, name, *args in schedule(bits, chunks):
        with region(name + "_".join(str(a) for a in args)):
            if where is None:
                parts[name](*args)
            else:
                pl.when(groups[where])(functools.partial(parts[name], *args))
    with region("qwait"):
        for c in range(chunks - LATE, chunks):
            q_late[c - chunks + LATE] = gathered(c)
    with region("sent"):
        rows = sum(sent) // (chunks * CHUNK)
        assert rows * chunks * CHUNK == sum(sent) and rows <= rows_dev
        everything = rbuf.at[:, pl.ds(0, rows)]
        pltpu.make_async_copy(everything, everything, send_sem.at[0]).wait()


def tree(bits, right_side, leaf_inverse, vt, ut, cores):
    rows_dev, cols = right_side.shape
    lf = leaf_inverse.shape[1]
    levels, rank = vt.shape[:2]
    blocks = rows_dev // lf
    chunks = cols // CHUNK
    local_levels = list(range(bits, levels))
    assert blocks == 2 ** len(local_levels) and bits >= 2
    gram_cols = pl.cdiv(rank * (bits - 1), LANES) * LANES
    depth = lf + pl.cdiv(rank * len(local_levels), LANES) * LANES
    wide = pl.cdiv(rank * bits, LANES) * LANES
    out_shape = [
        jax.ShapeDtypeStruct((chunks, rows_dev, CHUNK), F32),
        jax.ShapeDtypeStruct((LATE, rank * bits, CHUNK), F32),
        jax.ShapeDtypeStruct((rows_dev, wide), BF16),
        jax.ShapeDtypeStruct((rows_dev, wide), BF16),
    ]
    hbm = pl.BlockSpec(memory_space=pltpu.HBM)
    vmem = pl.BlockSpec(memory_space=pltpu.VMEM)
    counts = [2 ** (level - bits) for level in local_levels]
    rest = rank * (bits - 1)
    scratch = [
        pltpu.VMEM((chunks, rows_dev, CHUNK), F32),
        pltpu.VMEM((rows_dev, lf), F32),
        pltpu.VMEM((levels, rank, rows_dev), F32),
        pltpu.VMEM((levels, rank, rows_dev), F32),
        pltpu.VMEM((bits, 2 * rank, 2 * rank), F32),
        pltpu.SemaphoreType.DMA((6 + len(local_levels) + chunks,)),
        pltpu.VMEM((chunks, rows_dev, CHUNK), BF16),
        pltpu.VMEM((chunks, rows_dev, CHUNK), BF16),
        pltpu.VMEM((rows_dev, depth), BF16),
        pltpu.VMEM((rows_dev, depth), BF16),
        pltpu.VMEM((blocks, levels * rank, lf), BF16),
        pltpu.VMEM((blocks, levels * rank, lf), BF16),
        pltpu.VMEM((chunks, max(rank * (2 * blocks - 2), rank), CHUNK), BF16),
        pltpu.VMEM((chunks, max(rank * (2 * blocks - 2), rank), CHUNK), BF16),
        pltpu.VMEM((bits, rank * (bits + 1), 2 * rank), BF16),
        pltpu.VMEM((bits, rank * (bits + 1), 2 * rank), BF16),
        pltpu.VMEM((bits - 1, rest, gram_cols), F32),
        pltpu.VMEM((bits - 1, rest, gram_cols), F32),
        pltpu.VMEM((chunks, rank * bits, LANES), F32),
        pltpu.VMEM((chunks, rank * bits, LANES), F32),
        pltpu.VMEM((chunks, rank * bits, LANES), F32),
        pltpu.VMEM((bits, chunks, rest, LANES), F32),
        pltpu.VMEM((bits, chunks, rest, LANES), F32),
        pltpu.VMEM((bits, chunks, rank, LANES), F32),
        pltpu.VMEM((chunks, 2, rank * bits, LANES), F32),
        pltpu.SemaphoreType.DMA((bits - 1,)),
        pltpu.SemaphoreType.DMA((chunks,)),
        pltpu.SemaphoreType.DMA((bits - 1, chunks)),
        pltpu.SemaphoreType.DMA((chunks,)),
        pltpu.VMEM((2, rank, LANES), F32),
        pltpu.SemaphoreType.DMA((2,)),
        pltpu.SemaphoreType.DMA((1,)),
    ]
    scratch += [pltpu.VMEM((count, 2 * rank, 2 * rank), F32) for count in counts]
    scratch += [
        pltpu.VMEM((count, rank * (level + 2), 2 * rank), BF16)
        for count, level in zip(counts, local_levels)
        for _ in range(2)
    ]
    return pl.pallas_call(
        functools.partial(tree_kernel, bits, levels, blocks),
        out_shape=out_shape,
        in_specs=[hbm] * 5,
        out_specs=[vmem] * 4,
        scratch_shapes=scratch,
        compiler_params=pltpu.CompilerParams(
            collective_id=0, has_side_effects=True, vmem_limit_bytes=TREE_VMEM + 32 * rows_dev * lf
        ),
        name="tree",
    )(right_side, leaf_inverse, vt, ut, cores)


def finish_kernel(x_ref, q_ref, uh_ref, ul_ref, out_hbm, last, sems):
    chunks, rows_dev, width = x_ref.shape
    copies = []

    def write(src, rows, c):
        dst = out_hbm.at[pl.ds(rows, src.shape[0]), pl.ds(c * width, width)]
        copy = pltpu.make_async_copy(src, dst, sems.at[len(copies)])
        copy.start()
        copies.append(copy)

    late = q_ref.shape[0]
    for c in range(chunks - late):
        write(x_ref.at[c], 0, c)
    piece = rows_dev // PIECES
    for n in range(late):
        q = q_ref[n]
        pad = uh_ref.shape[1] - q.shape[0]
        if pad:
            q = jnp.concatenate([q, jnp.zeros((pad, width), F32)], 0)
        q = split(q)
        c = chunks - late + n
        for start in range(0, rows_dev, piece):
            rows = slice(start, start + piece)
            last[n, rows] = x_ref[c, rows] + dot3((uh_ref[rows], ul_ref[rows]), q)
            write(last.at[n, pl.ds(start, piece)], start, c)
    for copy in copies:
        copy.wait()


def finish(x, q, u_high, u_low):
    chunks, rows_dev, width = x.shape
    vmem = pl.BlockSpec(memory_space=pltpu.VMEM)
    return pl.pallas_call(
        finish_kernel,
        out_shape=jax.ShapeDtypeStruct((rows_dev, chunks * width), F32),
        in_specs=[vmem] * 4,
        out_specs=pl.BlockSpec(memory_space=pltpu.HBM),
        scratch_shapes=[
            pltpu.VMEM((q.shape[0], rows_dev, width), F32),
            pltpu.SemaphoreType.DMA((chunks + q.shape[0] * (PIECES - 1),)),
        ],
        compiler_params=pltpu.CompilerParams(vmem_limit_bytes=FINISH_VMEM),
        name="finish",
    )(x, q, u_high, u_low)


def local(bits, right_side, leaf_inverse, left_factors, right_factors, cores):
    ut = jnp.swapaxes(left_factors, 1, 2)
    vt = jnp.swapaxes(right_factors, 1, 2)
    right_side, leaf_inverse, vt, ut, cores = (
        pltpu.with_memory_space_constraint(a, pltpu.HBM)
        for a in (right_side, leaf_inverse, vt, ut, cores)
    )
    return finish(*tree(bits, right_side, leaf_inverse, vt, ut, cores))


def solution(mesh):
    bits = mesh.shape["rows"].bit_length() - 1
    in_specs = (
        P(("rep", "rows"), None),
        P(("rep", "rows"), None),
        P(None, ("rep", "rows"), None),
        P(None, ("rep", "rows"), None),
        P("rep", None, None),
    )
    out_specs = P(("rep", "rows"), None)
    return jax.shard_map(
        functools.partial(local, bits),
        mesh=mesh,
        in_specs=in_specs,
        out_specs=out_specs,
        check_vma=False,
    )
```

```python
import contextlib
import functools

import jax
import jax.numpy as jnp
from jax import lax
from jax.experimental import pallas as pl
from jax.experimental.pallas import tpu as pltpu
from jax.sharding import PartitionSpec as P

LANES = 128
CHUNK = 2 * LANES
F32 = jnp.float32
BF16 = jnp.bfloat16
TREE_VMEM = 24 << 20
FINISH_VMEM = 12 << 20
MESH = pl.DeviceIdType.MESH
TRACE = False
LATE = 2
PIECES = 2
CROSS = True


def region(name):
    return jax.named_scope(name) if TRACE else contextlib.nullcontext()


def split(x):
    high = x.astype(BF16)
    return high, (x - high.astype(F32)).astype(BF16)


def level_order(bits, levels):
    return [bits - 1 - s for s in range(bits)] + list(range(bits, levels))


def local_offset(level, bits, rank):
    return rank * (2 ** (level - bits + 1) - 2)


def one(x, y, nt=False):
    dims = (((1,), (1 if nt else 0,)), ((), ()))
    return lax.dot_general(x, y, dims, preferred_element_type=F32)


def dot3(a, b, nt=False):
    return one(a[0], b[0], nt) + one(a[0], b[1], nt) + one(a[1], b[0], nt)


def dotk(a, b):
    return one(
        jnp.concatenate([a[0], a[0], a[1]], 1), jnp.concatenate([b[0], b[1], b[0]], 0)
    )


def dot(a, b):
    return dotk(split(a), split(b))


def swap_lanes(x):
    half = x.shape[1] // 2
    return jnp.concatenate([x[:, half:], x[:, :half]], 1)


def schedule(bits, chunks):
    if bits == 3 and chunks == 4:
        return [
            (None, "forward", 0), (True, "bases"), (None, "forward", 1), (None, "forward", 2),
            (None, "operator", 0), (True, "leaves", 0), (None, "step", 0, 0),
            (None, "forward", 3), (None, "step", 0, 1), (None, "operator", 1), (False, "bases"),
            (None, "step", 1, 0), (None, "step", 0, 2), (False, "leaves", 3),
            (None, "step", 0, 3), (None, "give", 0, 0), (None, "give", 1, 0),
            (None, "give", 0, 1), (None, "step", 1, 1), (True, "leaves", 3), (False, "leaves", 2),
            (None, "give", 0, 2), (None, "give", 0, 3), (None, "give", 1, 1),
            (None, "operator", 2), (None, "step", 1, 2), (None, "step", 2, 0),
            (None, "give", 2, 0), (True, "leaves", 2), (False, "leaves", 1), (None, "step", 1, 3),
            (None, "give", 1, 2), (True, "leaves", 1), (False, "leaves", 0), (None, "step", 2, 1),
            (None, "give", 2, 1), (None, "give", 1, 3), ("early", "apply", 0),
            (None, "step", 2, 2), (None, "give", 2, 2), ("late", "apply", 0), (None, "apply", 1),
            (None, "step", 2, 3),
        ]
    order = [("forward", c) for c in range(chunks)]
    order += [("operator", s) for s in range(bits)] + [("bases",)]
    for t in range(chunks + bits - 1):
        for s in range(bits):
            if 0 <= t - s < chunks:
                order.append(("step", s, t - s))
                if not (CROSS and s == bits - 1 and t - s == chunks - 1):
                    order.append(("give", s, t - s))
        if t < chunks:
            order.append(("leaves", t))
    order += [("apply", c) for c in range(chunks - LATE)]
    return [(None, *item) for item in order]


def tree_kernel(bits, levels, blocks, right_hbm, leaf_hbm, vt_hbm, ut_hbm, cores_hbm, *refs):
    x_ref, q_late, u_high, u_low = refs[:4]
    rbuf, leaf, vt_ref, ut_ref, core_g, sem_in = refs[4:10]
    r_high, r_low, a_high, a_low, m_high, m_low, *both_refs = refs[10:18]
    op_high, op_low, gram_out, gram_in, keep, first_out, first_in = refs[18:25]
    later_out, later_in, q_out, q_all = refs[25:29]
    gram_sem, first_sem, later_sem, q_sem = refs[29:33]
    last_in, last_sem, send_sem = refs[33:36]
    local_levels = list(range(bits, levels))
    core_l = refs[36 : 36 + len(local_levels)]
    ch_refs = refs[36 + len(local_levels) :]
    ch_refs = list(zip(ch_refs[::2], ch_refs[1::2]))

    me = lax.axis_index("rows")
    rank, rows_dev = vt_ref.shape[1:]
    chunks = rbuf.shape[0]
    lf = rows_dev // blocks
    half_id = lax.rem(me, 2)
    upper = half_id == 1
    order = level_order(bits, levels)
    gram_cols = gram_out.shape[2]
    second = lax.rem(lax.axis_index("rep"), 2) == 1

    def child(s):
        return lax.rem(me // 2**s, 2)

    def partner(s):
        return me + (1 - 2 * child(s)) * 2**s

    cross = partner(bits - 1) + (1 - 2 * child(0))
    greeted = [partner(s) for s in range(bits)]
    barrier = pltpu.get_barrier_semaphore()
    for target in greeted:
        pl.semaphore_signal(barrier, inc=1, device_id={"rows": target}, device_id_type=MESH)

    slots = [0]

    def load(src, dst):
        copy = pltpu.make_async_copy(src, dst, sem_in.at[slots[0]])
        slots[0] += 1
        copy.start()
        return copy

    pieces = 2 if blocks % 2 == 0 else 1
    width = rows_dev // pieces
    v_loads, leaf_loads = [], []
    for n in range(pieces):
        part = pl.ds(n * width, width)
        v_loads.append(load(vt_hbm.at[:, :, part], vt_ref.at[:, :, part]))
        leaf_loads.append(load(leaf_hbm.at[part], leaf.at[part]))
    u_load = load(ut_hbm, ut_ref)
    core_loads = []
    for n, level in enumerate(local_levels):
        count = 2 ** (level - bits)
        src = cores_hbm.at[pl.ds(2**level - 1 + me * count, count)]
        core_loads.append(load(src, core_l[n]))
    right_loads = {0: load(right_hbm.at[:, pl.ds(0, CHUNK)], rbuf.at[0])}
    for c in range(1, chunks):
        src = right_hbm.at[:, pl.ds(c * CHUNK, CHUNK)]
        pltpu.make_async_copy(src, rbuf.at[c], sem_in.at[slots[0]]).start()
    others = rbuf.at[pl.ds(1, chunks - 1)]
    right_loads[1] = pltpu.make_async_copy(others, others, sem_in.at[slots[0]])
    slots[0] += 1
    for s in range(bits):
        src = cores_hbm.at[2 ** (bits - 1 - s) - 1 + me // 2 ** (s + 1)]
        pltpu.make_async_copy(src, core_g.at[s], sem_in.at[slots[0]]).start()
    core_g_load = pltpu.make_async_copy(core_g, core_g, sem_in.at[slots[0]])

    sent = []

    def send(src, dst, sem, target):
        copy = pltpu.make_async_remote_copy(
            src_ref=src,
            dst_ref=dst,
            send_sem=send_sem.at[0],
            recv_sem=sem,
            device_id={"rows": target},
            device_id_type=MESH,
        )
        copy.start()
        sent.append(src.shape[0] * src.shape[1])
        return copy

    vt = []
    for n in range(pieces):
        part = slice(n * width, (n + 1) * width)
        with region(f"wait_v{n}"):
            v_loads[n].wait()
        v = split(jnp.concatenate([vt_ref[level, :, part] for level in order], 0))
        vt.append(v)
        with region(f"wait_leaf{n}"):
            leaf_loads[n].wait()
        with region(f"m{n}"):
            high, low = split(leaf[part])
            a_high[part, :lf] = high
            a_low[part, :lf] = low
            for i in range(n * blocks // pieces, (n + 1) * blocks // pieces):
                rows = slice(i * lf, (i + 1) * lf)
                cols = slice(i * lf - n * width, (i + 1) * lf - n * width)
                high, low = split(dot3([x[:, cols] for x in v], (a_high[rows, :lf], a_low[rows, :lf])))
                m_high[i] = high
                m_low[i] = low
    vt = [jnp.concatenate(x, 1) for x in zip(*vt)]
    with region("wait_u"):
        u_load.wait()
        for copy in core_loads:
            copy.wait()

    def set_local(n, k, gram):
        core = core_l[n][k]
        for ref, top, rest in zip(ch_refs[n], split(core), split(dot(gram, core))):
            ref[k, : 2 * rank] = top
            ref[k, 2 * rank :] = rest

    with region("grams"):
        fast = len(local_levels) == 2 and bits == 3 and 2 * rank == LANES
        if fast:
            ut = {level: split(ut_ref[level]) for level in range(1, levels)}
            rows_v = rank * (levels - 1)
            lane = lax.broadcasted_iota(jnp.int32, (rows_v, LANES), 1) < rank
            tile_a, tile_b = [], []
            for i in range(blocks):
                cols = slice(i * lf, (i + 1) * lf)
                names = [4, 2] if i % 2 == 0 else [2, 4]
                names += [3, 1] if i < 2 else [1, 3]
                rhs = [
                    jnp.concatenate([ut[level][j][:, cols] for level in names], 0)
                    for j in range(2)
                ]
                g = dot3([v[:rows_v, cols] for v in vt], rhs, nt=True)
                tile_a.append(g[:, :LANES])
                tile_b.append(g[:, LANES:])
            s01, s23 = tile_b[0] + tile_b[1], tile_b[2] + tile_b[3]
            even, odd = tile_a[0] + tile_a[2], tile_a[1] + tile_a[3]
            cut = slice(rank, rank * bits)
            gram_out[0] = jnp.where(
                lane[cut], odd[cut] + swap_lanes(even[cut]), s01[cut] + swap_lanes(s23[cut])
            )
        else:
            vr = [v[rank : rank * bits] for v in vt]
            ur = split(jnp.concatenate([ut_ref[level] for level in order], 0))
            gram_out[0] = dot3(vr, [u[:gram_cols] for u in ur], nt=True)
    with region("barrier"):
        pl.semaphore_wait(barrier, len(greeted))
    gram_copy = {0: send(gram_out.at[0], gram_in.at[0], gram_sem.at[0], partner(0))}
    with region("ch"):
        if fast:
            for k in range(2):
                set_local(1, k, jnp.where(lane, tile_a[2 * k], tile_a[2 * k + 1]))
            cut = slice(0, rank * bits)
            set_local(0, 0, jnp.where(lane[cut], s01[cut], s23[cut]))
        else:
            for n, level in enumerate(local_levels):
                count = 2 ** (level - bits)
                node = rows_dev // count
                half = node // 2
                zero = jnp.zeros((rank, half), BF16)
                own = slice(rank * level, rank * (level + 1))
                for k in range(count):
                    base = k * node
                    diag = [
                        jnp.concatenate(
                            [
                                jnp.concatenate([u[own, base : base + half], zero], 1),
                                jnp.concatenate([zero, u[own, base + half : base + node]], 1),
                            ],
                            0,
                        )
                        for u in ur
                    ]
                    above = [v[: rank * level, base : base + node] for v in vt]
                    set_local(n, k, dot3(above, diag, nt=True))

    first_copy, later_copy, last_copy = {}, {}, []

    def forward(c):
        if c in right_loads:
            right_loads[c].wait()
        high, low = split(rbuf[c])
        r_high[c] = high
        r_low[c] = low
        parts = []
        for i in range(blocks):
            rows = slice(i * lf, (i + 1) * lf)
            parts.append(dot3((m_high[i], m_low[i]), (r_high[c, rows, :], r_low[c, rows, :])))
        for n in reversed(range(len(local_levels))):
            level = local_levels[n]
            top = rank * level
            merged = []
            for k in range(len(parts) // 2):
                a, b = parts[2 * k], parts[2 * k + 1]
                both = split(jnp.concatenate([b[top:], a[top:]], 0))
                change = dotk([ref[k, 2 * rank :] for ref in ch_refs[n]], both)
                start = local_offset(level, bits, rank) + 2 * rank * k
                for ref, value in zip(both_refs, both):
                    ref[c, start : start + 2 * rank] = value
                merged.append(a[:top] + b[:top] - change)
            parts = merged
        p = parts[0]
        low, high = p[:, :LANES], p[:, LANES:]
        first_out[c] = jnp.where(upper, low, high)
        first_copy[c] = send(first_out.at[c], first_in.at[c], first_sem.at[c], partner(0))
        keep[c] = jnp.where(upper, high, low)

    def bases():
        def turned(rows, width):
            extra = width - rank * len(rows)
            if extra:
                rows = rows + [jnp.zeros((extra, rows_dev), F32)]
            return split(-jnp.concatenate(rows, 0).T)

        if local_levels:
            high, low = turned([ut_ref[level] for level in local_levels], a_high.shape[1] - lf)
            a_high[:, lf:] = high
            a_low[:, lf:] = low
        high, low = turned([ut_ref[bits - 1 - s] for s in range(bits)], u_high.shape[1])
        u_high[...] = high
        u_low[...] = low

    def leaves(c):
        images = []
        for n, level in enumerate(local_levels):
            for k in range(2 ** (level - bits)):
                start = local_offset(level, bits, rank) + 2 * rank * k
                both = [ref[c, start : start + 2 * rank] for ref in both_refs]
                images.append(split(dotk([ref[k, : 2 * rank] for ref in ch_refs[n]], both)))
        for i in range(blocks):
            rows = slice(i * lf, (i + 1) * lf)
            highs, lows = [r_high[c, rows, :]], [r_low[c, rows, :]]
            width = lf
            for level in local_levels:
                place = rank * (i * 2 ** (level - bits + 1) // blocks)
                start = local_offset(level, bits, rank) + place
                high, low = images[start // (2 * rank)]
                part = slice(start % (2 * rank), start % (2 * rank) + rank)
                highs.append(high[part])
                lows.append(low[part])
                width += rank
            if a_high.shape[1] > width:
                zero = jnp.zeros((a_high.shape[1] - width, CHUNK), BF16)
                highs.append(zero)
                lows.append(zero)
            x_ref[c, rows, :] = dotk(
                (a_high[rows, :], a_low[rows, :]),
                (jnp.concatenate(highs, 0), jnp.concatenate(lows, 0)),
            )

    def operator(s):
        if s == 0:
            core_g_load.wait()
        first = child(s) == 0
        core = core_g[s]
        own = jnp.where(first, core[:rank], core[rank:])
        sib = jnp.where(first, core[rank:], core[:rank])
        parts = [own, sib] if s == 0 else [own]
        if s < bits - 1:
            gram_copy[s].wait_recv()
            rows = slice(rank * s, None)
            if s + 1 < bits - 1:
                gram_out[s + 1] = gram_out[s] + gram_in[s]
                gram_copy[s + 1] = send(
                    gram_out.at[s + 1],
                    gram_in.at[s + 1],
                    gram_sem.at[s + 1],
                    partner(s + 1),
                )
            before = [jnp.zeros((rank, 2 * rank), F32)] * s
            after = [jnp.zeros((rank, 2 * rank), F32)] * (gram_cols // rank - 1 - s)
            parts.append(
                -(
                    dot(gram_out[s, rows, :], jnp.concatenate(before + [own] + after, 0))
                    + dot(gram_in[s, rows, :], jnp.concatenate(before + [sib] + after, 0))
                )
            )
        whole = jnp.concatenate(parts, 0)
        high, low = split(jnp.where(first, swap_lanes(whole), whole))
        op_high[s, : high.shape[0]] = high
        op_low[s, : low.shape[0]] = low

    def crossed(s, c):
        return CROSS and s == bits - 1 and c == chunks - 1

    def halves(c, rows, value):
        q_all[c, 0, rows] = value[:, :LANES]
        q_all[c, 1, rows] = value[:, LANES:]

    def join(here, there):
        return jnp.concatenate(
            [jnp.where(upper, there, here), jnp.where(upper, here, there)], 1
        )

    def step(s, c):
        if s == 0:
            first_copy[c].wait_recv()
            mine, theirs = keep[c], first_in[c]
        else:
            later_copy[s, c].wait_recv()
            mine, theirs = later_out[s, c, rank * (s - 1) :], later_in[s, c, rank * (s - 1) :]
        if crossed(s, c):
            for copy in last_copy:
                copy.wait_recv()
            mine, theirs = join(mine, last_in[0]), join(theirs, last_in[1])
        count = rank * (bits - 1 - s) + (2 * rank if s == 0 else rank)
        both = split(jnp.concatenate([mine[:rank], theirs[:rank]], 0))
        image = dotk((op_high[s, :count], op_low[s, :count]), both)
        own = slice(rank * s, rank * (s + 1))
        if crossed(s, c):
            halves(c, own, image)
            return
        if s < bits - 1:
            later_out[s + 1, c, rank * s :] = (
                mine[rank:] + theirs[rank:] + image[count - rank * (bits - 1 - s) :]
            )
            part = pl.ds(rank * s, rank * (bits - 1 - s))
            later_copy[s + 1, c] = send(
                later_out.at[s + 1, c, part],
                later_in.at[s + 1, c, part],
                later_sem.at[s, c],
                partner(s + 1),
            )
            if crossed(s + 1, c):
                root = later_out.at[s + 1, c, pl.ds(rank * s, rank)]
                last_copy.append(send(root, last_in.at[1], last_sem.at[1], cross))
                last_copy.append(send(root, last_in.at[0], last_sem.at[0], partner(0)))
        q_out[s, c] = image[rank : 2 * rank] if s == 0 else image[:rank]
        q_all[c, half_id, own] = image[:rank]

    def give(s, c):
        place = q_all.at[c, half_id, pl.ds(rank * s, rank)]
        send(q_out.at[s, c], place, q_sem.at[c], partner(0))

    def gathered(c):
        given = q_all.at[c, 0, pl.ds(0, rank * (bits - 1 if crossed(bits - 1, c) else bits))]
        pltpu.make_async_copy(given, given, q_sem.at[c]).wait()
        return jnp.concatenate([q_all[c, 0], q_all[c, 1]], 1)

    def apply(c):
        q = gathered(c)
        pad = u_high.shape[1] - q.shape[0]
        if pad:
            q = jnp.concatenate([q, jnp.zeros((pad, CHUNK), F32)], 0)
        x_ref[c] = x_ref[c] + dot3((u_high[...], u_low[...]), split(q))

    parts = {f.__name__: f for f in (forward, operator, bases, step, give, leaves, apply)}
    early = (child(bits - 1) == 0) & (child(0) == 0)
    groups = {True: second, False: ~second, "late": ~early, "early": early}
    for where, name, *args in schedule(bits, chunks):
        with region(name + "_".join(str(a) for a in args)):
            if where is None:
                parts[name](*args)
            else:
                pl.when(groups[where])(functools.partial(parts[name], *args))
    with region("qwait"):
        for c in range(chunks - LATE, chunks):
            q_late[c - chunks + LATE] = gathered(c)
    with region("sent"):
        rows = sum(sent) // (chunks * CHUNK)
        assert rows * chunks * CHUNK == sum(sent) and rows <= rows_dev
        everything = rbuf.at[:, pl.ds(0, rows)]
        pltpu.make_async_copy(everything, everything, send_sem.at[0]).wait()


def tree(bits, right_side, leaf_inverse, vt, ut, cores):
    rows_dev, cols = right_side.shape
    lf = leaf_inverse.shape[1]
    levels, rank = vt.shape[:2]
    blocks = rows_dev // lf
    chunks = cols // CHUNK
    local_levels = list(range(bits, levels))
    assert blocks == 2 ** len(local_levels) and bits >= 2
    gram_cols = pl.cdiv(rank * (bits - 1), LANES) * LANES
    depth = lf + pl.cdiv(rank * len(local_levels), LANES) * LANES
    wide = pl.cdiv(rank * bits, LANES) * LANES
    out_shape = [
        jax.ShapeDtypeStruct((chunks, rows_dev, CHUNK), F32),
        jax.ShapeDtypeStruct((LATE, rank * bits, CHUNK), F32),
        jax.ShapeDtypeStruct((rows_dev, wide), BF16),
        jax.ShapeDtypeStruct((rows_dev, wide), BF16),
    ]
    hbm = pl.BlockSpec(memory_space=pltpu.HBM)
    vmem = pl.BlockSpec(memory_space=pltpu.VMEM)
    counts = [2 ** (level - bits) for level in local_levels]
    rest = rank * (bits - 1)
    scratch = [
        pltpu.VMEM((chunks, rows_dev, CHUNK), F32),
        pltpu.VMEM((rows_dev, lf), F32),
        pltpu.VMEM((levels, rank, rows_dev), F32),
        pltpu.VMEM((levels, rank, rows_dev), F32),
        pltpu.VMEM((bits, 2 * rank, 2 * rank), F32),
        pltpu.SemaphoreType.DMA((8 + len(local_levels),)),
        pltpu.VMEM((chunks, rows_dev, CHUNK), BF16),
        pltpu.VMEM((chunks, rows_dev, CHUNK), BF16),
        pltpu.VMEM((rows_dev, depth), BF16),
        pltpu.VMEM((rows_dev, depth), BF16),
        pltpu.VMEM((blocks, levels * rank, lf), BF16),
        pltpu.VMEM((blocks, levels * rank, lf), BF16),
        pltpu.VMEM((chunks, max(rank * (2 * blocks - 2), rank), CHUNK), BF16),
        pltpu.VMEM((chunks, max(rank * (2 * blocks - 2), rank), CHUNK), BF16),
        pltpu.VMEM((bits, rank * (bits + 1), 2 * rank), BF16),
        pltpu.VMEM((bits, rank * (bits + 1), 2 * rank), BF16),
        pltpu.VMEM((bits - 1, rest, gram_cols), F32),
        pltpu.VMEM((bits - 1, rest, gram_cols), F32),
        pltpu.VMEM((chunks, rank * bits, LANES), F32),
        pltpu.VMEM((chunks, rank * bits, LANES), F32),
        pltpu.VMEM((chunks, rank * bits, LANES), F32),
        pltpu.VMEM((bits, chunks, rest, LANES), F32),
        pltpu.VMEM((bits, chunks, rest, LANES), F32),
        pltpu.VMEM((bits, chunks, rank, LANES), F32),
        pltpu.VMEM((chunks, 2, rank * bits, LANES), F32),
        pltpu.SemaphoreType.DMA((bits - 1,)),
        pltpu.SemaphoreType.DMA((chunks,)),
        pltpu.SemaphoreType.DMA((bits - 1, chunks)),
        pltpu.SemaphoreType.DMA((chunks,)),
        pltpu.VMEM((2, rank, LANES), F32),
        pltpu.SemaphoreType.DMA((2,)),
        pltpu.SemaphoreType.DMA((1,)),
    ]
    scratch += [pltpu.VMEM((count, 2 * rank, 2 * rank), F32) for count in counts]
    scratch += [
        pltpu.VMEM((count, rank * (level + 2), 2 * rank), BF16)
        for count, level in zip(counts, local_levels)
        for _ in range(2)
    ]
    return pl.pallas_call(
        functools.partial(tree_kernel, bits, levels, blocks),
        out_shape=out_shape,
        in_specs=[hbm] * 5,
        out_specs=[vmem] * 4,
        scratch_shapes=scratch,
        compiler_params=pltpu.CompilerParams(
            collective_id=0, has_side_effects=True, vmem_limit_bytes=TREE_VMEM + 32 * rows_dev * lf
        ),
        name="tree",
    )(right_side, leaf_inverse, vt, ut, cores)


def finish_kernel(x_ref, q_ref, uh_ref, ul_ref, out_hbm, last, sem):
    chunks, rows_dev, width = x_ref.shape

    def write(src, rows, c):
        dst = out_hbm.at[pl.ds(rows, src.shape[0]), pl.ds(c * width, width)]
        pltpu.make_async_copy(src, dst, sem.at[0]).start()

    late = q_ref.shape[0]
    for c in range(chunks - late):
        write(x_ref.at[c], 0, c)
    piece = rows_dev // PIECES
    for n in range(late):
        q = q_ref[n]
        pad = uh_ref.shape[1] - q.shape[0]
        if pad:
            q = jnp.concatenate([q, jnp.zeros((pad, width), F32)], 0)
        q = split(q)
        c = chunks - late + n
        for start in range(0, rows_dev, piece):
            rows = slice(start, start + piece)
            last[n, rows] = x_ref[c, rows] + dot3((uh_ref[rows], ul_ref[rows]), q)
            write(last.at[n, pl.ds(start, piece)], start, c)
    pltpu.make_async_copy(x_ref, x_ref, sem.at[0]).wait()


def finish(x, q, u_high, u_low):
    chunks, rows_dev, width = x.shape
    vmem = pl.BlockSpec(memory_space=pltpu.VMEM)
    return pl.pallas_call(
        finish_kernel,
        out_shape=jax.ShapeDtypeStruct((rows_dev, chunks * width), F32),
        in_specs=[vmem] * 4,
        out_specs=pl.BlockSpec(memory_space=pltpu.HBM),
        scratch_shapes=[
            pltpu.VMEM((q.shape[0], rows_dev, width), F32),
            pltpu.SemaphoreType.DMA((1,)),
        ],
        compiler_params=pltpu.CompilerParams(vmem_limit_bytes=FINISH_VMEM),
        name="finish",
    )(x, q, u_high, u_low)


def local(bits, right_side, leaf_inverse, left_factors, right_factors, cores):
    ut = jnp.swapaxes(left_factors, 1, 2)
    vt = jnp.swapaxes(right_factors, 1, 2)
    right_side, leaf_inverse, vt, ut, cores = (
        pltpu.with_memory_space_constraint(a, pltpu.HBM)
        for a in (right_side, leaf_inverse, vt, ut, cores)
    )
    return finish(*tree(bits, right_side, leaf_inverse, vt, ut, cores))


def solution(mesh):
    bits = mesh.shape["rows"].bit_length() - 1
    in_specs = (
        P(("rep", "rows"), None),
        P(("rep", "rows"), None),
        P(None, ("rep", "rows"), None),
        P(None, ("rep", "rows"), None),
        P("rep", None, None),
    )
    out_specs = P(("rep", "rows"), None)
    return jax.shard_map(
        functools.partial(local, bits),
        mesh=mesh,
        in_specs=in_specs,
        out_specs=out_specs,
        check_vma=False,
    )
```

```python
import contextlib
import functools

import jax
import jax.numpy as jnp
from jax import lax
from jax.experimental import pallas as pl
from jax.experimental.pallas import tpu as pltpu
from jax.sharding import PartitionSpec as P

LANES = 128
CHUNK = 2 * LANES
F32 = jnp.float32
BF16 = jnp.bfloat16
TREE_VMEM = 24 << 20
FINISH_VMEM = 12 << 20
MESH = pl.DeviceIdType.MESH
TRACE = False
LATE = 2
PIECES = 2
CROSS = True


def region(name):
    return jax.named_scope(name) if TRACE else contextlib.nullcontext()


def split(x):
    high = x.astype(BF16)
    return high, (x - high.astype(F32)).astype(BF16)


def level_order(bits, levels):
    return [bits - 1 - s for s in range(bits)] + list(range(bits, levels))


def local_offset(level, bits, rank):
    return rank * (2 ** (level - bits + 1) - 2)


def one(x, y, nt=False):
    dims = (((1,), (1 if nt else 0,)), ((), ()))
    return lax.dot_general(x, y, dims, preferred_element_type=F32)


def dot3(a, b, nt=False):
    return one(a[0], b[0], nt) + one(a[0], b[1], nt) + one(a[1], b[0], nt)


def dotk(a, b):
    return one(
        jnp.concatenate([a[0], a[0], a[1]], 1), jnp.concatenate([b[0], b[1], b[0]], 0)
    )


def dot(a, b):
    return dotk(split(a), split(b))


def swap_lanes(x):
    half = x.shape[1] // 2
    return jnp.concatenate([x[:, half:], x[:, :half]], 1)


def schedule(bits, chunks):
    if bits == 3 and chunks == 4:
        return [
            (None, "forward", 0), (True, "bases"), (None, "forward", 1), (None, "operator", 0),
            (True, "leaves", 0), (None, "forward", 2), (None, "step", 0, 0), (None, "forward", 3),
            (None, "give", 0, 0), (None, "step", 0, 1), (None, "operator", 1), (False, "bases"),
            (None, "step", 1, 0), (None, "step", 0, 2), (False, "leaves", 3),
            (None, "step", 0, 3), (None, "give", 1, 0), (None, "give", 0, 1),
            (None, "step", 1, 1), (True, "leaves", 3), (False, "leaves", 2), (None, "give", 0, 2),
            (None, "give", 1, 1), (None, "give", 0, 3), (None, "operator", 2),
            (None, "step", 1, 2), (None, "give", 1, 2), (None, "step", 2, 0),
            (None, "give", 2, 0), (True, "leaves", 2), (False, "leaves", 1), (None, "step", 1, 3),
            (True, "leaves", 1), (False, "leaves", 0), (None, "step", 2, 1), (None, "give", 2, 1),
            (None, "give", 1, 3), ("early", "apply", 0), (None, "step", 2, 2),
            (None, "give", 2, 2), ("late", "apply", 0), (None, "apply", 1), (None, "step", 2, 3),
        ]
    order = [("forward", c) for c in range(chunks)]
    order += [("operator", s) for s in range(bits)] + [("bases",)]
    for t in range(chunks + bits - 1):
        for s in range(bits):
            if 0 <= t - s < chunks:
                order.append(("step", s, t - s))
                if not (CROSS and s == bits - 1 and t - s == chunks - 1):
                    order.append(("give", s, t - s))
        if t < chunks:
            order.append(("leaves", t))
    order += [("apply", c) for c in range(chunks - LATE)]
    return [(None, *item) for item in order]


def tree_kernel(bits, levels, blocks, right_hbm, leaf_hbm, vt_hbm, ut_hbm, cores_hbm, *refs):
    x_ref, q_late, u_high, u_low = refs[:4]
    rbuf, leaf, vt_ref, ut_ref, core_g, sem_in = refs[4:10]
    r_high, r_low, a_high, a_low, m_high, m_low, *both_refs = refs[10:18]
    op_high, op_low, gram_out, gram_in, keep, first_out, first_in = refs[18:25]
    later_out, later_in, q_out, q_all = refs[25:29]
    gram_sem, first_sem, later_sem, q_sem = refs[29:33]
    last_in, last_sem, send_sem = refs[33:36]
    local_levels = list(range(bits, levels))
    core_l = refs[36 : 36 + len(local_levels)]
    ch_refs = refs[36 + len(local_levels) :]
    ch_refs = list(zip(ch_refs[::2], ch_refs[1::2]))

    me = lax.axis_index("rows")
    rank, rows_dev = vt_ref.shape[1:]
    chunks = rbuf.shape[0]
    lf = rows_dev // blocks
    half_id = lax.rem(me, 2)
    upper = half_id == 1
    order = level_order(bits, levels)
    gram_cols = gram_out.shape[2]
    second = lax.rem(lax.axis_index("rep"), 2) == 1

    def child(s):
        return lax.rem(me // 2**s, 2)

    def partner(s):
        return me + (1 - 2 * child(s)) * 2**s

    cross = partner(bits - 1) + (1 - 2 * child(0))
    greeted = [partner(s) for s in range(bits)]
    barrier = pltpu.get_barrier_semaphore()
    for target in greeted:
        pl.semaphore_signal(barrier, inc=1, device_id={"rows": target}, device_id_type=MESH)

    slots = [0]

    def load(src, dst):
        copy = pltpu.make_async_copy(src, dst, sem_in.at[slots[0]])
        slots[0] += 1
        copy.start()
        return copy

    pieces = 2 if blocks % 2 == 0 else 1
    width = rows_dev // pieces
    v_loads, leaf_loads = [], []
    for n in range(pieces):
        part = pl.ds(n * width, width)
        v_loads.append(load(vt_hbm.at[:, :, part], vt_ref.at[:, :, part]))
        leaf_loads.append(load(leaf_hbm.at[part], leaf.at[part]))
    u_load = load(ut_hbm, ut_ref)
    core_loads = []
    for n, level in enumerate(local_levels):
        count = 2 ** (level - bits)
        src = cores_hbm.at[pl.ds(2**level - 1 + me * count, count)]
        core_loads.append(load(src, core_l[n]))
    right_loads = [
        load(right_hbm.at[:, pl.ds(c * CHUNK, CHUNK)], rbuf.at[c]) for c in range(chunks)
    ]
    for s in range(bits):
        src = cores_hbm.at[2 ** (bits - 1 - s) - 1 + me // 2 ** (s + 1)]
        pltpu.make_async_copy(src, core_g.at[s], sem_in.at[slots[0]]).start()
    core_g_load = pltpu.make_async_copy(core_g, core_g, sem_in.at[slots[0]])

    sent = []

    def send(src, dst, sem, target):
        copy = pltpu.make_async_remote_copy(
            src_ref=src,
            dst_ref=dst,
            send_sem=send_sem.at[0],
            recv_sem=sem,
            device_id={"rows": target},
            device_id_type=MESH,
        )
        copy.start()
        sent.append(src.shape[0] * src.shape[1])
        return copy

    vt = []
    for n in range(pieces):
        part = slice(n * width, (n + 1) * width)
        with region(f"wait_v{n}"):
            v_loads[n].wait()
        v = split(jnp.concatenate([vt_ref[level, :, part] for level in order], 0))
        vt.append(v)
        with region(f"wait_leaf{n}"):
            leaf_loads[n].wait()
        with region(f"m{n}"):
            high, low = split(leaf[part])
            a_high[part, :lf] = high
            a_low[part, :lf] = low
            for i in range(n * blocks // pieces, (n + 1) * blocks // pieces):
                rows = slice(i * lf, (i + 1) * lf)
                cols = slice(i * lf - n * width, (i + 1) * lf - n * width)
                high, low = split(dot3([x[:, cols] for x in v], (a_high[rows, :lf], a_low[rows, :lf])))
                m_high[i] = high
                m_low[i] = low
    vt = [jnp.concatenate(x, 1) for x in zip(*vt)]
    with region("wait_u"):
        u_load.wait()
        for copy in core_loads:
            copy.wait()

    def set_local(n, k, gram):
        core = core_l[n][k]
        for ref, top, rest in zip(ch_refs[n], split(core), split(dot(gram, core))):
            ref[k, : 2 * rank] = top
            ref[k, 2 * rank :] = rest

    with region("grams"):
        fast = len(local_levels) == 2 and bits == 3 and 2 * rank == LANES
        if fast:
            ut = {level: split(ut_ref[level]) for level in range(1, levels)}
            rows_v = rank * (levels - 1)
            lane = lax.broadcasted_iota(jnp.int32, (rows_v, LANES), 1) < rank
            tile_a, tile_b = [], []
            for i in range(blocks):
                cols = slice(i * lf, (i + 1) * lf)
                names = [4, 2] if i % 2 == 0 else [2, 4]
                names += [3, 1] if i < 2 else [1, 3]
                rhs = [
                    jnp.concatenate([ut[level][j][:, cols] for level in names], 0)
                    for j in range(2)
                ]
                g = dot3([v[:rows_v, cols] for v in vt], rhs, nt=True)
                tile_a.append(g[:, :LANES])
                tile_b.append(g[:, LANES:])
            s01, s23 = tile_b[0] + tile_b[1], tile_b[2] + tile_b[3]
            even, odd = tile_a[0] + tile_a[2], tile_a[1] + tile_a[3]
            cut = slice(rank, rank * bits)
            gram_out[0] = jnp.where(
                lane[cut], odd[cut] + swap_lanes(even[cut]), s01[cut] + swap_lanes(s23[cut])
            )
        else:
            vr = [v[rank : rank * bits] for v in vt]
            ur = split(jnp.concatenate([ut_ref[level] for level in order], 0))
            gram_out[0] = dot3(vr, [u[:gram_cols] for u in ur], nt=True)
    with region("barrier"):
        pl.semaphore_wait(barrier, len(greeted))
    gram_copy = {0: send(gram_out.at[0], gram_in.at[0], gram_sem.at[0], partner(0))}
    with region("ch"):
        if fast:
            for k in range(2):
                set_local(1, k, jnp.where(lane, tile_a[2 * k], tile_a[2 * k + 1]))
            cut = slice(0, rank * bits)
            set_local(0, 0, jnp.where(lane[cut], s01[cut], s23[cut]))
        else:
            for n, level in enumerate(local_levels):
                count = 2 ** (level - bits)
                node = rows_dev // count
                half = node // 2
                zero = jnp.zeros((rank, half), BF16)
                own = slice(rank * level, rank * (level + 1))
                for k in range(count):
                    base = k * node
                    diag = [
                        jnp.concatenate(
                            [
                                jnp.concatenate([u[own, base : base + half], zero], 1),
                                jnp.concatenate([zero, u[own, base + half : base + node]], 1),
                            ],
                            0,
                        )
                        for u in ur
                    ]
                    above = [v[: rank * level, base : base + node] for v in vt]
                    set_local(n, k, dot3(above, diag, nt=True))

    first_copy, later_copy, last_copy = {}, {}, []

    def forward(c):
        right_loads[c].wait()
        high, low = split(rbuf[c])
        r_high[c] = high
        r_low[c] = low
        parts = []
        for i in range(blocks):
            rows = slice(i * lf, (i + 1) * lf)
            parts.append(dot3((m_high[i], m_low[i]), (r_high[c, rows, :], r_low[c, rows, :])))
        for n in reversed(range(len(local_levels))):
            level = local_levels[n]
            top = rank * level
            merged = []
            for k in range(len(parts) // 2):
                a, b = parts[2 * k], parts[2 * k + 1]
                both = split(jnp.concatenate([b[top:], a[top:]], 0))
                change = dotk([ref[k, 2 * rank :] for ref in ch_refs[n]], both)
                start = local_offset(level, bits, rank) + 2 * rank * k
                for ref, value in zip(both_refs, both):
                    ref[c, start : start + 2 * rank] = value
                merged.append(a[:top] + b[:top] - change)
            parts = merged
        p = parts[0]
        low, high = p[:, :LANES], p[:, LANES:]
        first_out[c] = jnp.where(upper, low, high)
        first_copy[c] = send(first_out.at[c], first_in.at[c], first_sem.at[c], partner(0))
        keep[c] = jnp.where(upper, high, low)

    def bases():
        def turned(rows, width):
            extra = width - rank * len(rows)
            if extra:
                rows = rows + [jnp.zeros((extra, rows_dev), F32)]
            return split(-jnp.concatenate(rows, 0).T)

        if local_levels:
            high, low = turned([ut_ref[level] for level in local_levels], a_high.shape[1] - lf)
            a_high[:, lf:] = high
            a_low[:, lf:] = low
        high, low = turned([ut_ref[bits - 1 - s] for s in range(bits)], u_high.shape[1])
        u_high[...] = high
        u_low[...] = low

    def leaves(c):
        images = []
        for n, level in enumerate(local_levels):
            for k in range(2 ** (level - bits)):
                start = local_offset(level, bits, rank) + 2 * rank * k
                both = [ref[c, start : start + 2 * rank] for ref in both_refs]
                images.append(split(dotk([ref[k, : 2 * rank] for ref in ch_refs[n]], both)))
        for i in range(blocks):
            rows = slice(i * lf, (i + 1) * lf)
            highs, lows = [r_high[c, rows, :]], [r_low[c, rows, :]]
            width = lf
            for level in local_levels:
                place = rank * (i * 2 ** (level - bits + 1) // blocks)
                start = local_offset(level, bits, rank) + place
                high, low = images[start // (2 * rank)]
                part = slice(start % (2 * rank), start % (2 * rank) + rank)
                highs.append(high[part])
                lows.append(low[part])
                width += rank
            if a_high.shape[1] > width:
                zero = jnp.zeros((a_high.shape[1] - width, CHUNK), BF16)
                highs.append(zero)
                lows.append(zero)
            x_ref[c, rows, :] = dotk(
                (a_high[rows, :], a_low[rows, :]),
                (jnp.concatenate(highs, 0), jnp.concatenate(lows, 0)),
            )

    def operator(s):
        if s == 0:
            core_g_load.wait()
        first = child(s) == 0
        core = core_g[s]
        own = jnp.where(first, core[:rank], core[rank:])
        sib = jnp.where(first, core[rank:], core[:rank])
        parts = [own, sib] if s == 0 else [own]
        if s < bits - 1:
            gram_copy[s].wait_recv()
            rows = slice(rank * s, None)
            if s + 1 < bits - 1:
                gram_out[s + 1] = gram_out[s] + gram_in[s]
                gram_copy[s + 1] = send(
                    gram_out.at[s + 1],
                    gram_in.at[s + 1],
                    gram_sem.at[s + 1],
                    partner(s + 1),
                )
            before = [jnp.zeros((rank, 2 * rank), F32)] * s
            after = [jnp.zeros((rank, 2 * rank), F32)] * (gram_cols // rank - 1 - s)
            parts.append(
                -(
                    dot(gram_out[s, rows, :], jnp.concatenate(before + [own] + after, 0))
                    + dot(gram_in[s, rows, :], jnp.concatenate(before + [sib] + after, 0))
                )
            )
        whole = jnp.concatenate(parts, 0)
        high, low = split(jnp.where(first, swap_lanes(whole), whole))
        op_high[s, : high.shape[0]] = high
        op_low[s, : low.shape[0]] = low

    def crossed(s, c):
        return CROSS and s == bits - 1 and c == chunks - 1

    def halves(c, rows, value):
        q_all[c, 0, rows] = value[:, :LANES]
        q_all[c, 1, rows] = value[:, LANES:]

    def join(here, there):
        return jnp.concatenate(
            [jnp.where(upper, there, here), jnp.where(upper, here, there)], 1
        )

    def step(s, c):
        if s == 0:
            first_copy[c].wait_recv()
            mine, theirs = keep[c], first_in[c]
        else:
            later_copy[s, c].wait_recv()
            mine, theirs = later_out[s, c, rank * (s - 1) :], later_in[s, c, rank * (s - 1) :]
        if crossed(s, c):
            for copy in last_copy:
                copy.wait_recv()
            mine, theirs = join(mine, last_in[0]), join(theirs, last_in[1])
        count = rank * (bits - 1 - s) + (2 * rank if s == 0 else rank)
        both = split(jnp.concatenate([mine[:rank], theirs[:rank]], 0))
        image = dotk((op_high[s, :count], op_low[s, :count]), both)
        own = slice(rank * s, rank * (s + 1))
        if crossed(s, c):
            halves(c, own, image)
            return
        if s < bits - 1:
            later_out[s + 1, c, rank * s :] = (
                mine[rank:] + theirs[rank:] + image[count - rank * (bits - 1 - s) :]
            )
            part = pl.ds(rank * s, rank * (bits - 1 - s))
            later_copy[s + 1, c] = send(
                later_out.at[s + 1, c, part],
                later_in.at[s + 1, c, part],
                later_sem.at[s, c],
                partner(s + 1),
            )
            if crossed(s + 1, c):
                root = later_out.at[s + 1, c, pl.ds(rank * s, rank)]
                last_copy.append(send(root, last_in.at[1], last_sem.at[1], cross))
                last_copy.append(send(root, last_in.at[0], last_sem.at[0], partner(0)))
        q_out[s, c] = image[rank : 2 * rank] if s == 0 else image[:rank]
        q_all[c, half_id, own] = image[:rank]

    def give(s, c):
        place = q_all.at[c, half_id, pl.ds(rank * s, rank)]
        send(q_out.at[s, c], place, q_sem.at[c], partner(0))

    def gathered(c):
        given = q_all.at[c, 0, pl.ds(0, rank * (bits - 1 if crossed(bits - 1, c) else bits))]
        pltpu.make_async_copy(given, given, q_sem.at[c]).wait()
        return jnp.concatenate([q_all[c, 0], q_all[c, 1]], 1)

    def apply(c):
        q = gathered(c)
        pad = u_high.shape[1] - q.shape[0]
        if pad:
            q = jnp.concatenate([q, jnp.zeros((pad, CHUNK), F32)], 0)
        x_ref[c] = x_ref[c] + dot3((u_high[...], u_low[...]), split(q))

    parts = {f.__name__: f for f in (forward, operator, bases, step, give, leaves, apply)}
    early = (child(bits - 1) == 0) & (child(0) == 0)
    groups = {True: second, False: ~second, "late": ~early, "early": early}
    for where, name, *args in schedule(bits, chunks):
        with region(name + "_".join(str(a) for a in args)):
            if where is None:
                parts[name](*args)
            else:
                pl.when(groups[where])(functools.partial(parts[name], *args))
    with region("qwait"):
        for c in range(chunks - LATE, chunks):
            q_late[c - chunks + LATE] = gathered(c)
    with region("sent"):
        rows = sum(sent) // (chunks * CHUNK)
        assert rows * chunks * CHUNK == sum(sent) and rows <= rows_dev
        everything = rbuf.at[:, pl.ds(0, rows)]
        pltpu.make_async_copy(everything, everything, send_sem.at[0]).wait()


def tree(bits, right_side, leaf_inverse, vt, ut, cores):
    rows_dev, cols = right_side.shape
    lf = leaf_inverse.shape[1]
    levels, rank = vt.shape[:2]
    blocks = rows_dev // lf
    chunks = cols // CHUNK
    local_levels = list(range(bits, levels))
    assert blocks == 2 ** len(local_levels) and bits >= 2
    gram_cols = pl.cdiv(rank * (bits - 1), LANES) * LANES
    depth = lf + pl.cdiv(rank * len(local_levels), LANES) * LANES
    wide = pl.cdiv(rank * bits, LANES) * LANES
    out_shape = [
        jax.ShapeDtypeStruct((chunks, rows_dev, CHUNK), F32),
        jax.ShapeDtypeStruct((LATE, rank * bits, CHUNK), F32),
        jax.ShapeDtypeStruct((rows_dev, wide), BF16),
        jax.ShapeDtypeStruct((rows_dev, wide), BF16),
    ]
    hbm = pl.BlockSpec(memory_space=pltpu.HBM)
    vmem = pl.BlockSpec(memory_space=pltpu.VMEM)
    counts = [2 ** (level - bits) for level in local_levels]
    rest = rank * (bits - 1)
    scratch = [
        pltpu.VMEM((chunks, rows_dev, CHUNK), F32),
        pltpu.VMEM((rows_dev, lf), F32),
        pltpu.VMEM((levels, rank, rows_dev), F32),
        pltpu.VMEM((levels, rank, rows_dev), F32),
        pltpu.VMEM((bits, 2 * rank, 2 * rank), F32),
        pltpu.SemaphoreType.DMA((6 + len(local_levels) + chunks,)),
        pltpu.VMEM((chunks, rows_dev, CHUNK), BF16),
        pltpu.VMEM((chunks, rows_dev, CHUNK), BF16),
        pltpu.VMEM((rows_dev, depth), BF16),
        pltpu.VMEM((rows_dev, depth), BF16),
        pltpu.VMEM((blocks, levels * rank, lf), BF16),
        pltpu.VMEM((blocks, levels * rank, lf), BF16),
        pltpu.VMEM((chunks, max(rank * (2 * blocks - 2), rank), CHUNK), BF16),
        pltpu.VMEM((chunks, max(rank * (2 * blocks - 2), rank), CHUNK), BF16),
        pltpu.VMEM((bits, rank * (bits + 1), 2 * rank), BF16),
        pltpu.VMEM((bits, rank * (bits + 1), 2 * rank), BF16),
        pltpu.VMEM((bits - 1, rest, gram_cols), F32),
        pltpu.VMEM((bits - 1, rest, gram_cols), F32),
        pltpu.VMEM((chunks, rank * bits, LANES), F32),
        pltpu.VMEM((chunks, rank * bits, LANES), F32),
        pltpu.VMEM((chunks, rank * bits, LANES), F32),
        pltpu.VMEM((bits, chunks, rest, LANES), F32),
        pltpu.VMEM((bits, chunks, rest, LANES), F32),
        pltpu.VMEM((bits, chunks, rank, LANES), F32),
        pltpu.VMEM((chunks, 2, rank * bits, LANES), F32),
        pltpu.SemaphoreType.DMA((bits - 1,)),
        pltpu.SemaphoreType.DMA((chunks,)),
        pltpu.SemaphoreType.DMA((bits - 1, chunks)),
        pltpu.SemaphoreType.DMA((chunks,)),
        pltpu.VMEM((2, rank, LANES), F32),
        pltpu.SemaphoreType.DMA((2,)),
        pltpu.SemaphoreType.DMA((1,)),
    ]
    scratch += [pltpu.VMEM((count, 2 * rank, 2 * rank), F32) for count in counts]
    scratch += [
        pltpu.VMEM((count, rank * (level + 2), 2 * rank), BF16)
        for count, level in zip(counts, local_levels)
        for _ in range(2)
    ]
    return pl.pallas_call(
        functools.partial(tree_kernel, bits, levels, blocks),
        out_shape=out_shape,
        in_specs=[hbm] * 5,
        out_specs=[vmem] * 4,
        scratch_shapes=scratch,
        compiler_params=pltpu.CompilerParams(
            collective_id=0, has_side_effects=True, vmem_limit_bytes=TREE_VMEM + 32 * rows_dev * lf
        ),
        name="tree",
    )(right_side, leaf_inverse, vt, ut, cores)


def finish_kernel(x_ref, q_ref, uh_ref, ul_ref, out_hbm, last, sems):
    chunks, rows_dev, width = x_ref.shape
    copies = []

    def write(src, rows, c):
        dst = out_hbm.at[pl.ds(rows, src.shape[0]), pl.ds(c * width, width)]
        copy = pltpu.make_async_copy(src, dst, sems.at[len(copies)])
        copy.start()
        copies.append(copy)

    late = q_ref.shape[0]
    for c in range(chunks - late):
        write(x_ref.at[c], 0, c)
    piece = rows_dev // PIECES
    for n in range(late):
        q = q_ref[n]
        pad = uh_ref.shape[1] - q.shape[0]
        if pad:
            q = jnp.concatenate([q, jnp.zeros((pad, width), F32)], 0)
        q = split(q)
        c = chunks - late + n
        for start in range(0, rows_dev, piece):
            rows = slice(start, start + piece)
            last[n, rows] = x_ref[c, rows] + dot3((uh_ref[rows], ul_ref[rows]), q)
            write(last.at[n, pl.ds(start, piece)], start, c)
    for copy in copies:
        copy.wait()


def finish(x, q, u_high, u_low):
    chunks, rows_dev, width = x.shape
    vmem = pl.BlockSpec(memory_space=pltpu.VMEM)
    return pl.pallas_call(
        finish_kernel,
        out_shape=jax.ShapeDtypeStruct((rows_dev, chunks * width), F32),
        in_specs=[vmem] * 4,
        out_specs=pl.BlockSpec(memory_space=pltpu.HBM),
        scratch_shapes=[
            pltpu.VMEM((q.shape[0], rows_dev, width), F32),
            pltpu.SemaphoreType.DMA((chunks + q.shape[0] * (PIECES - 1),)),
        ],
        compiler_params=pltpu.CompilerParams(vmem_limit_bytes=FINISH_VMEM),
        name="finish",
    )(x, q, u_high, u_low)


def local(bits, right_side, leaf_inverse, left_factors, right_factors, cores):
    ut = jnp.swapaxes(left_factors, 1, 2)
    vt = jnp.swapaxes(right_factors, 1, 2)
    right_side, leaf_inverse, vt, ut, cores = (
        pltpu.with_memory_space_constraint(a, pltpu.HBM)
        for a in (right_side, leaf_inverse, vt, ut, cores)
    )
    return finish(*tree(bits, right_side, leaf_inverse, vt, ut, cores))


def solution(mesh):
    bits = mesh.shape["rows"].bit_length() - 1
    in_specs = (
        P(("rep", "rows"), None),
        P(("rep", "rows"), None),
        P(None, ("rep", "rows"), None),
        P(None, ("rep", "rows"), None),
        P("rep", None, None),
    )
    out_specs = P(("rep", "rows"), None)
    return jax.shard_map(
        functools.partial(local, bits),
        mesh=mesh,
        in_specs=in_specs,
        out_specs=out_specs,
        check_vma=False,
    )
```
